512 devices in a mesh: body: 32 (over y, x), surf: 16 (over z, core).
Axes of the slice: x: 4, y: 8, z: 8, core: 2. Of those that a mesh axis runs over, the one named last changes fastest.
Arguments:
- body_panels: float32 [12, 96, 2048], P(None, 'body', 'surf'), may hold values from -6 to 192, as said below
- body_normals: float32 [3, 96, 2048], P(None, 'body', 'surf'), may hold values from -3 to 3
- fs_panels: float32 [4, 65536], P(None, ('body', 'surf')), may hold values from -6 to 192, as said below
- fs_state: float32 [2, 65536], P(None, ('body', 'surf')), may hold values from -6 to 6
- pairs: int32 [72, 2], replicated, may hold values from 0 to 95, as said below
Outputs:
- body_potential: float32 [96, 8, 2048], P('body', None, 'surf')
- body_force: float32 [96, 8, 3], P('body')
- fs_next: float32 [2, 65536], P(None, ('body', 'surf'))
The draws below stay inside these ranges and needn't reach their ends.
Inputs may be any that keep to these rules, and one draw needn't show every extreme that they name: Rows are distinct pairs (i, j) with i < j <= i + 3, ordered by i and then by j. `body_panels`: body b's centroids lie within x in 2 b - 1 to 2 b + 1, y in -1 to 1, z in -2 to -1; areas are positive; source strengths are within -6 to 6. `fs_panels`: Free-surface panels of group g have x in 2 * 3 g - 1 to 2 * 3 (g + 1) - 1, y in -3 to 3, positive areas, source strengths within -6 to 6.
All inputs are finite; a program needn't handle non-finite values.
Results may differ from the reference program's by a relative error of at most 0.0003.
Values sent between devices are 32-bit elements; how exact they have to be, the bound alone decides.
A program may use at most 64 MiB of HBM per device.

```python
import math
import jax
import jax.numpy as jnp
from jax import lax

P_SIZE = 2048
SETS = 8
BODY_DEV = 3
FS = 2048
BODIES = 96
FS_ALL = 65536
NPAIRS = 72


def draw_body_panels(key, part):
    key_place, key_area, key_source = jax.random.split(key, 3)
    spread = jax.random.uniform(key_place, (3, BODIES, P_SIZE), jnp.float32, -1.0, 1.0)
    centre = 2.0 * jnp.arange(BODIES, dtype=jnp.float32)[:, None]
    coord_x = centre + spread[0]
    coord_y = spread[1]
    coord_z = -1.5 + 0.5 * spread[2]
    area = jax.random.uniform(key_area, (1, BODIES, P_SIZE), jnp.float32, 0.5, 1.5) * (4.0 / math.sqrt(P_SIZE))
    source = jnp.clip(jax.random.normal(key_source, (SETS, BODIES, P_SIZE), jnp.float32), -6.0, 6.0)
    return jnp.concatenate([coord_x[None], coord_y[None], coord_z[None], area, source], axis=0)


def draw_fs_panels(key, part):
    key_x, key_y, key_source, key_area = jax.random.split(key, 4)
    group = (jnp.arange(FS_ALL, dtype=jnp.int32) // FS).astype(jnp.float32)
    span = 2.0 * BODY_DEV
    coord_x = span * group + span * jax.random.uniform(key_x, (FS_ALL,), jnp.float32, 0.0, 1.0) - 1.0
    coord_y = jax.random.uniform(key_y, (FS_ALL,), jnp.float32, -3.0, 3.0)
    source = jnp.clip(jax.random.normal(key_source, (FS_ALL,), jnp.float32), -6.0, 6.0)
    area = jax.random.uniform(key_area, (FS_ALL,), jnp.float32, 0.5, 1.5) * (4.0 / math.sqrt(FS))
    return jnp.stack([coord_x, coord_y, source, area])


def draw_pairs(key, part):
    candidate_count = BODIES * BODY_DEV
    candidate = jnp.arange(candidate_count, dtype=jnp.int32)
    first_body = candidate // BODY_DEV
    reach_step = candidate % BODY_DEV + 1
    valid = first_body + reach_step < BODIES
    scores = jax.random.randint(key, (candidate_count,), 0, 1024, dtype=jnp.int32) * candidate_count + candidate + 2
    forced = (candidate == 0) | (candidate == (BODIES - 2) * BODY_DEV)
    scores = jnp.where(forced, candidate - candidate_count, scores)
    scores = jnp.where(valid, scores, 1025 * candidate_count + candidate + 2)
    chosen = jnp.sort(jnp.argsort(scores)[:NPAIRS])
    return jnp.stack([first_body[chosen], first_body[chosen] + reach_step[chosen]], axis=1).astype(jnp.int32)


def steps_of(own_key, extent, cuts, least, top_value):
    level, own = 1.0, jax.random.fold_in(own_key, 6)
    for position, blocks in cuts:
        heights = jnp.exp(jax.random.uniform(jax.random.fold_in(own, position), (blocks,), jnp.float32, least / len(cuts), top_value / len(cuts)))
        level = level * jnp.repeat(heights, extent[position] // blocks).reshape([-1 if axis == position else 1 for axis in range(len(extent))])
    return level


def noise(stream_key, shape, deviation, most, cuts=(), held_as=jnp.bfloat16):
    values = deviation * jax.random.normal(stream_key, shape, jnp.float32)
    if cuts:
        values = values * steps_of(stream_key, shape, cuts, -0.22, 0.18)
    return jnp.clip(values, -most, most).astype(held_as)


def setup_inputs(seed: int = 0) -> dict:
    arg_keys = jax.random.split(jax.random.key(seed), 6)
    return {
        "body_panels": draw_body_panels(jax.random.fold_in(arg_keys[5], 71), 0),
        "body_normals": noise(arg_keys[1], (3, BODIES, P_SIZE), 0.6, 3.0, ((1, 32), (2, 16)), jnp.float32),
        "fs_panels": draw_fs_panels(jax.random.fold_in(arg_keys[5], 71), 0),
        "fs_state": noise(arg_keys[3], (2, FS_ALL), 1.0, 6.0, ((1, 512),), jnp.float32),
        "pairs": draw_pairs(jax.random.fold_in(arg_keys[5], 71), 0),
    }


soften = 0.01
gravity = 9.81
time_step = 0.2
highest = lax.Precision.HIGHEST

def kernel_block(targets, sources):
    delta_x = targets[0][:, None] - sources[0][None, :]
    delta_y = targets[1][:, None] - sources[1][None, :]
    delta_z = targets[2][:, None] - sources[2][None, :]
    return lax.rsqrt(delta_x * delta_x + delta_y * delta_y + delta_z * delta_z + soften)

def reference(body_panels, body_normals, fs_panels, fs_state, pairs):
    points = body_panels[:3]
    weights = body_panels[4:] * body_panels[3][None]

    def self_term(body_id):
        body_points = lax.dynamic_index_in_dim(points, body_id, 1, keepdims=False)
        body_weights = lax.dynamic_index_in_dim(weights, body_id, 1, keepdims=False)
        influence = kernel_block(body_points, body_points)
        return lax.dot_general(body_weights, influence, (((1,), (1,)), ((), ())), precision=highest)
    potential = lax.map(self_term, jnp.arange(BODIES, dtype=jnp.int32))

    def pair_step(acc_potential, pair_row):
        first_body = pair_row[0]
        second_body = pair_row[1]
        first_points = lax.dynamic_index_in_dim(points, first_body, 1, keepdims=False)
        second_points = lax.dynamic_index_in_dim(points, second_body, 1, keepdims=False)
        first_weights = lax.dynamic_index_in_dim(weights, first_body, 1, keepdims=False)
        second_weights = lax.dynamic_index_in_dim(weights, second_body, 1, keepdims=False)
        influence = kernel_block(first_points, second_points)
        to_first = lax.dot_general(second_weights, influence, (((1,), (1,)), ((), ())), precision=highest)
        to_second = jnp.dot(first_weights, influence, precision=highest)
        acc_potential = acc_potential.at[first_body].add(to_first)
        acc_potential = acc_potential.at[second_body].add(to_second)
        return (acc_potential, None)
    potential, unused = lax.scan(pair_step, potential, pairs)
    groups = BODIES // BODY_DEV
    fs_points = jnp.stack([fs_panels[0], fs_panels[1], jnp.zeros_like(fs_panels[0])])
    fs_weights = fs_panels[2] * fs_panels[3]

    def group_term(group_id):
        group_points = lax.dynamic_slice_in_dim(points, group_id * BODY_DEV, BODY_DEV, 1).reshape(3, BODY_DEV * P_SIZE)
        group_weights = lax.dynamic_slice_in_dim(weights[0], group_id * BODY_DEV, BODY_DEV, 0).reshape(BODY_DEV * P_SIZE)
        surface_points = lax.dynamic_slice_in_dim(fs_points, group_id * FS, FS, 1)
        surface_weights = lax.dynamic_slice_in_dim(fs_weights, group_id * FS, FS, 0)
        delta_x = surface_points[0][None, :] - group_points[0][:, None]
        delta_y = surface_points[1][None, :] - group_points[1][:, None]
        delta_z = surface_points[2][None, :] - group_points[2][:, None]
        inverse = lax.rsqrt(delta_x * delta_x + delta_y * delta_y + delta_z * delta_z + soften)
        from_surface = jnp.dot(inverse, surface_weights, precision=highest).reshape(BODY_DEV, P_SIZE)
        cubed = inverse * inverse * inverse
        velocity = -jnp.stack([jnp.dot(group_weights, delta_x * cubed, precision=highest), jnp.dot(group_weights, delta_y * cubed, precision=highest), jnp.dot(group_weights, delta_z * cubed, precision=highest)])
        return (from_surface, velocity)
    from_surface, velocity = lax.map(group_term, jnp.arange(groups, dtype=jnp.int32))
    potential = potential.at[:, 0].add(from_surface.reshape(BODIES, P_SIZE))
    area_normals = body_normals * body_panels[3][None]
    force = jnp.einsum('cbp,bsp->bsc', area_normals, potential, precision=highest)
    velocity = velocity.transpose(1, 0, 2).reshape(3, FS_ALL)
    speed_sq = velocity[0] * velocity[0] + velocity[1] * velocity[1] + velocity[2] * velocity[2]
    next_potential = fs_state[0] + time_step * (-gravity * fs_state[1] - 0.5 * speed_sq)
    next_elevation = fs_state[1] + time_step * velocity[2]
    return (potential, force, jnp.stack([next_potential, next_elevation]))
```

```python
import functools

import jax
import jax.numpy as jnp
from jax import lax
from jax.experimental import pallas as pl
from jax.experimental.pallas import tpu as pltpu
from jax.sharding import PartitionSpec as P

MESH = pl.DeviceIdType.MESH
F32 = jnp.float32
BF16 = jnp.bfloat16
SOFTEN = 0.01
GRAVITY = 9.81
STEP = 0.2
DEPTH = 1.5

CROSS = [
    [(+1, t) for t in range(b + 1)] + [(-1, t) for t in range(b, 3)] for b in range(3)
]
PAIRS = [(0, 1), (0, 2), (1, 2)]
PAIRS += [(b, 3 + t) for b in range(3) for t in range(b + 1)]
PAIRS += [(t - 3, b) for b in range(3) for t in range(b, 3)]


def rounded(x):
    return x.astype(BF16).astype(F32)


def split3(x):
    a = rounded(x)
    r = x - a
    b = rounded(r)
    return a, b, rounded(r - b)


def split2(x):
    a = rounded(x)
    return jnp.concatenate([a, x - a], axis=0).astype(BF16)


def kernel(
    nz,
    bp, bn, fsp, fst, prs,
    pot, force, fsn,
    pay, nbr, tgt, tgf, ft, acc, accf, reto, reti, msk, frc,
    s_dir, r_dir, s_rel, r_rel, s_nb, r_nb, s_ret, r_ret, s_f, r_f,
):
    groups = lax.axis_size("body")
    tiles = 2 * nz
    g = lax.axis_index("body")
    s = lax.axis_index("surf")
    z, core = s // 2, lax.rem(s, 2)
    partner = 2 * z + 1 - core
    following = lax.rem(g + 1, groups)
    preceding = lax.rem(g + groups - 1, groups)

    barrier = pltpu.get_barrier_semaphore()
    for d in range(1, tiles):
        pl.semaphore_signal(
            barrier, inc=1, device_id=(g, lax.rem(s + d, tiles)), device_id_type=MESH
        )
    for other in (following, preceding):
        pl.semaphore_signal(barrier, inc=1, device_id=(other, s), device_id_type=MESH)

    base = 6.0 * g.astype(F32)
    area = bp[3]
    for k in range(8):
        w = bp[4 + k] * area
        for b in range(3):
            pay[0, 0, 8 * b + k : 8 * b + k + 1, :] = w[b : b + 1, :]
    for b in range(3):
        x = bp[0, b : b + 1, :] - (base + 2.0 * b)
        y = bp[1, b : b + 1, :]
        zz = bp[2, b : b + 1, :] + DEPTH
        for i, v in enumerate((x, y, zz, x * x + y * y + zz * zz)):
            pay[0, 0, 24 + 4 * b + i : 25 + 4 * b + i, :] = v
    fx = fsp[0:1, :] - (base + 2.0)
    fy = fsp[1:2, :]
    for i, v in enumerate((fx, fy, fsp[2:3, :] * fsp[3:4, :], fx * fx + fy * fy)):
        pay[0, 0, 36 + i : 37 + i, :] = v

    pl.semaphore_wait(barrier, tiles + 1)

    def direct(o):
        return pltpu.make_async_remote_copy(
            src_ref=pay.at[0, 0], dst_ref=pay.at[o, 0],
            send_sem=s_dir.at[o], recv_sem=r_dir.at[o],
            device_id=(g, 2 * lax.rem(z + o, nz) + core), device_id_type=MESH,
        )

    def relay(o):
        return pltpu.make_async_remote_copy(
            src_ref=pay.at[o, 0], dst_ref=pay.at[o, 1],
            send_sem=s_rel.at[o], recv_sem=r_rel.at[o],
            device_id=(g, partner), device_id_type=MESH,
        )

    def points(i):
        return pltpu.make_async_remote_copy(
            src_ref=pay.at[0, 0, pl.ds(24, 16)], dst_ref=nbr.at[i],
            send_sem=s_nb.at[i], recv_sem=r_nb.at[i],
            device_id=((following, preceding)[i], s), device_id_type=MESH,
        )

    def give_back(i):
        return pltpu.make_async_remote_copy(
            src_ref=reto.at[i], dst_ref=reti.at[i],
            send_sem=s_ret.at[i], recv_sem=r_ret.at[i],
            device_id=((following, preceding)[i], s), device_id_type=MESH,
        )

    def forces(d, slot):
        return pltpu.make_async_remote_copy(
            src_ref=frc.at[slot], dst_ref=frc.at[slot],
            send_sem=s_f.at[d], recv_sem=r_f.at[slot],
            device_id=(g, lax.rem(s + d, tiles)), device_id_type=MESH,
        )

    def order(k):
        half = (k + 1) // 2
        return jnp.where(lax.rem(k, 2) == 1, half, lax.rem(nz - half, nz))

    points(0).start()
    points(1).start()
    relay(0).start()
    for h in range(1, nz // 2 + 1):
        direct(h).start()
        if h != nz - h:
            direct(nz - h).start()

    row_i = lax.broadcasted_iota(jnp.int32, (16, prs.shape[1]), 0)
    first = jnp.full(row_i.shape, -9, jnp.int32)
    second = first
    for r, (i, j) in enumerate(PAIRS):
        first = jnp.where(row_i == r, i, first)
        second = jnp.where(row_i == r, j, second)
    found = (prs[0:1, :] == first + 3 * g) & (prs[1:2, :] == second + 3 * g)
    hit = jnp.sum(jnp.where(found, 1.0, 0.0), axis=1, keepdims=True)
    msk[...] = jnp.broadcast_to(hit, (16, 128))

    def allowed(i, j):
        r = PAIRS.index((i, j))
        return jnp.broadcast_to(msk[r : r + 1, :], (8, 128))

    row8 = lax.broadcasted_iota(jnp.int32, (8, 128), 0)

    def put_target(ref, at, x, y, zz, top, use_z=True):
        m = x * x + y * y + zz * zz + SOFTEN
        o = 0 if top else 4
        t = jnp.where(row8 == o, -2.0 * x, 0.0)
        t = jnp.where(row8 == o + 1, -2.0 * y, t)
        if use_z:
            t = jnp.where(row8 == o + 2, -2.0 * zz, t)
        t = jnp.where(row8 == o + 3, 1.0, t)
        t = jnp.where(row8 == 4 - o, m, t)
        t1, t2, t3 = split3(t)
        ref[:, 128 * at : 128 * at + 128] = jnp.concatenate(
            [t1, t2, t1, t2, t3, t1], axis=0
        ).astype(BF16)

    def spread(ref, r):
        return jnp.broadcast_to(ref[r : r + 1, :], (8, 128))

    def target(b, at, ref, r, shift):
        put_target(
            tgt.at[b], at, spread(ref, r) + 2.0 * shift, spread(ref, r + 1),
            spread(ref, r + 2), b != 1,
        )

    mine = pay.at[0, 0]
    for b in range(3):
        for t in range(3):
            target(b, 4 + t, mine, 24 + 4 * t, t - b)
        put_target(
            tgt.at[b], 7, spread(mine, 36) + 2.0 * (1 - b), spread(mine, 37),
            jnp.full((8, 128), DEPTH, F32), b != 1,
        )
    for t in range(3):
        put_target(
            tgf, t, spread(mine, 24 + 4 * t) + 2.0 * (t - 1), spread(mine, 25 + 4 * t),
            spread(mine, 26 + 4 * t) - DEPTH, False, use_z=False,
        )

    acc[...] = jnp.zeros_like(acc)
    accf[...] = jnp.zeros_like(accf)

    points(0).wait_recv()
    points(1).wait_recv()
    for b in range(3):
        for at, (side, t) in enumerate(CROSS[b]):
            target(b, at, nbr.at[0 if side < 0 else 1], 4 * t, 3 * side + t - b)

    row = lax.broadcasted_iota(jnp.int32, (8, 256), 0)

    def both(o, r):
        return jnp.concatenate([pay[o, 0, r : r + 8, :], pay[o, 1, r : r + 8, :]], axis=1)

    def sources(o):
        p, q = both(o, 24), both(o, 32)
        low = row < 4
        one4 = jnp.where(row == 4, 1.0, 0.0)
        one0 = jnp.where(row == 0, 1.0, 0.0)
        for i, c in enumerate(
            (jnp.where(low, p, one4), jnp.where(low, one0, p),
             jnp.where(low, q, one4), jnp.where(low, one0, q))
        ):
            c1, c2, c3 = split3(c)
            f = jnp.concatenate([c1, c1, c2, c2, c1, c3], axis=0)
            ft[o, i] = f.T.astype(BF16)

    def sweep(features, targets, lhs, cubed=False):
        total = None
        for c in range(2):
            rows = features[128 * c : 128 * c + 128, :]
            left = lhs[:, 128 * c : 128 * c + 128]
            d2 = jnp.dot(rows, targets, preferred_element_type=F32)
            k = lax.rsqrt(d2)
            if cubed:
                k = k * k * k
            hi = k.astype(BF16)
            lo = (k - hi.astype(F32)).astype(BF16)
            part = jnp.dot(left, hi, preferred_element_type=F32)
            part += jnp.dot(left, lo, preferred_element_type=F32)
            total = part if total is None else total + part
        return total

    def cross_step(k, carry):
        o = order(k)

        @pl.when(k < nz - 1)
        def _():
            ahead = order(k + 1)
            direct(ahead).wait_recv()
            relay(ahead).start()

        relay(o).wait_recv()
        sources(o)
        for b in range(3):
            lhs = split2(both(o, 8 * b))
            for n in (0, 256):
                acc[b, :, n : n + 256] += sweep(ft.at[o, b], tgt[b, :, n : n + 256], lhs)
        return carry

    lax.fori_loop(0, nz, cross_step, 0)

    def result(b, at):
        lanes = pl.ds(128 * at, 128)
        return acc[b, 0:8, lanes] + acc[b, 8:16, lanes]

    for i, side in enumerate((+1, -1)):
        for t in range(3):
            total = jnp.zeros((8, 128), F32)
            for b in range(3):
                if (side, t) in CROSS[b]:
                    pair = (b, 3 + t) if side > 0 else (t - 3, b)
                    total += result(b, CROSS[b].index((side, t))) * allowed(*pair)
            reto[i, t] = total
    give_back(0).start()
    give_back(1).start()

    def own_step(o, carry):
        for b in range(3):
            lhs = split2(both(o, 8 * b))
            for n, width in ((512, 256), (768, 128)):
                acc[b, :, n : n + width] += sweep(ft.at[o, b], tgt[b, :, n : n + width], lhs)
        lhs = split2(both(o, 32))
        for n, width in ((0, 256), (256, 128)):
            accf[:, n : n + width] += sweep(ft.at[o, 3], tgf[:, n : n + width], lhs)
        return carry

    lax.fori_loop(0, nz, own_step, 0)

    give_back(0).wait_recv()
    give_back(1).wait_recv()
    lane = lax.broadcasted_iota(jnp.int32, (8, 128), 1)
    packed = jnp.zeros((8, 128), F32)
    for t in range(3):
        total = reti[0, t] + reti[1, t]
        for b in range(3):
            r = result(b, 4 + t)
            total += r if b == t else r * allowed(min(b, t), max(b, t))
        surface = accf[6:7, 128 * t : 128 * t + 128] + accf[14:15, 128 * t : 128 * t + 128]
        total += jnp.where(row8 == 0, surface, 0.0)
        pot[t] = total
        for k in range(3):
            an = bn[k, t : t + 1, :] * bp[3, t : t + 1, :]
            column = jnp.sum(total * an, axis=1, keepdims=True)
            packed = jnp.where(lane == 16 * row8 + 3 * t + k, column, packed)
    frc[s] = jnp.sum(packed, axis=0, keepdims=True)
    for d in range(1, tiles):
        forces(d, s).start()

    def velocity_step(o, carry):
        for b in range(3):
            tile = both(o, 24 if b < 2 else 32)
            w0 = jnp.broadcast_to(both(o, 8 * b)[0:1, :], (8, 256))
            r = 4 if b == 1 else 0
            lhs = split2(w0 * jnp.where(row == r + 3, 1.0, tile))
            acc[b, :, 896:1024] += sweep(ft.at[o, b], tgt[b, :, 896:1024], lhs, cubed=True)
        return carry

    lax.fori_loop(0, nz, velocity_step, 0)

    v = [jnp.zeros((1, 128), F32)] * 3
    for b in range(3):
        moments = result(b, 7)
        r = 4 if b == 1 else 0
        point = (pay[0, 0, 36:37, :] + 2.0 * (1 - b), pay[0, 0, 37:38, :], DEPTH)
        for i in range(3):
            v[i] = v[i] + (moments[r + i : r + i + 1] - point[i] * moments[r + 3 : r + 4])
    speed_sq = v[0] * v[0] + v[1] * v[1] + v[2] * v[2]
    phi, eta = fst[0:1, :], fst[1:2, :]
    fsn[0:1, :] = phi + STEP * (-GRAVITY * eta - 0.5 * speed_sq)
    fsn[1:2, :] = eta + STEP * v[2]

    for d in range(1, tiles):
        forces(0, lax.rem(s + d, tiles)).wait_recv()
    whole = frc[0]
    for i in range(1, tiles):
        whole = whole + frc[i]
    whole = jnp.broadcast_to(whole, (8, 128))
    for t in range(3):
        for k in range(3):
            force[t, :, k : k + 1] = jnp.sum(
                jnp.where(lane == 16 * row8 + 3 * t + k, whole, 0.0), axis=1, keepdims=True
            )

    for i in range(2):
        points(i).wait_send()
        give_back(i).wait_send()
    for o in range(nz):
        relay(o).wait_send()
        if o:
            direct(o).wait_send()
    for d in range(1, tiles):
        forces(d, s).wait_send()


def on_device(bp, bn, fsp, fst, pairs):
    nz = lax.axis_size("surf") // 2
    tiles = 2 * nz
    dma = pltpu.SemaphoreType.DMA
    vmem = pl.BlockSpec(memory_space=pltpu.VMEM)
    return pl.pallas_call(
        functools.partial(kernel, nz),
        out_shape=(
            jax.ShapeDtypeStruct((3, 8, 128), F32),
            jax.ShapeDtypeStruct((3, 8, 3), F32),
            jax.ShapeDtypeStruct((2, 128), F32),
        ),
        in_specs=[vmem] * 5,
        out_specs=(vmem,) * 3,
        scratch_shapes=[
            pltpu.VMEM((nz, 2, 40, 128), F32),
            pltpu.VMEM((2, 16, 128), F32),
            pltpu.VMEM((3, 48, 1024), BF16),
            pltpu.VMEM((48, 384), BF16),
            pltpu.VMEM((nz, 4, 256, 48), BF16),
            pltpu.VMEM((3, 16, 1024), F32),
            pltpu.VMEM((16, 384), F32),
            pltpu.VMEM((2, 3, 8, 128), F32),
            pltpu.VMEM((2, 3, 8, 128), F32),
            pltpu.VMEM((16, 128), F32),
            pltpu.VMEM((tiles, 1, 128), F32),
            dma((nz,)), dma((nz,)), dma((nz,)), dma((nz,)),
            dma((2,)), dma((2,)), dma((2,)), dma((2,)),
            dma((tiles,)), dma((tiles,)),
        ],
        compiler_params=pltpu.CompilerParams(collective_id=0, has_side_effects=True),
        name="section",
    )(bp, bn, fsp, fst, pairs.T)


def solution(mesh):
    placed = (
        P(None, "body", "surf"),
        P(None, "body", "surf"),
        P(None, ("body", "surf")),
        P(None, ("body", "surf")),
        P(),
    )
    return jax.shard_map(
        on_device,
        mesh=mesh,
        in_specs=placed,
        out_specs=(P("body", None, "surf"), P("body", None, None), P(None, ("body", "surf"))),
        check_vma=False,
    )
```

```python
import functools

import jax
import jax.numpy as jnp
from jax import lax
from jax.experimental import pallas as pl
from jax.experimental.pallas import tpu as pltpu
from jax.sharding import PartitionSpec as P

MESH = pl.DeviceIdType.MESH
F32 = jnp.float32
BF16 = jnp.bfloat16
SOFTEN = 0.01
GRAVITY = 9.81
STEP = 0.2
DEPTH = 1.5

CROSS = [
    [(+1, t) for t in range(b + 1)] + [(-1, t) for t in range(b, 3)] for b in range(3)
]
PAIRS = [(0, 1), (0, 2), (1, 2)]
PAIRS += [(b, 3 + t) for b in range(3) for t in range(b + 1)]
PAIRS += [(t - 3, b) for b in range(3) for t in range(b, 3)]


def rounded(x):
    return x.astype(BF16).astype(F32)


def split3(x):
    a = rounded(x)
    r = x - a
    b = rounded(r)
    return a, b, rounded(r - b)


def split2(x):
    a = rounded(x)
    return jnp.concatenate([a, x - a], axis=0).astype(BF16)


def kernel(
    nz,
    bp, bn, fsp, fst, prs,
    pot, force, fsn,
    pay, nbr, tgt, tgp, tgf, tgv, ft, acc, accp, accf, accv, accw, reto, reti, msk, frc,
    s_dir, r_dir, s_rel, r_rel, s_nb, r_nb, s_ret, r_ret, s_f, r_f,
):
    groups = lax.axis_size("body")
    tiles = 2 * nz
    g = lax.axis_index("body")
    s = lax.axis_index("surf")
    z, core = s // 2, lax.rem(s, 2)
    partner = 2 * z + 1 - core
    following = lax.rem(g + 1, groups)
    preceding = lax.rem(g + groups - 1, groups)

    barrier = pltpu.get_barrier_semaphore()
    for d in range(1, tiles):
        pl.semaphore_signal(
            barrier, inc=1, device_id=(g, lax.rem(s + d, tiles)), device_id_type=MESH
        )
    for other in (following, preceding):
        pl.semaphore_signal(barrier, inc=1, device_id=(other, s), device_id_type=MESH)

    base = 6.0 * g.astype(F32)
    area = bp[3]
    for k in range(8):
        w = bp[4 + k] * area
        for b in range(3):
            pay[0, 0, 8 * b + k : 8 * b + k + 1, :] = w[b : b + 1, :]
    for b in range(3):
        x = bp[0, b : b + 1, :] - (base + 2.0 * b)
        y = bp[1, b : b + 1, :]
        zz = bp[2, b : b + 1, :] + DEPTH
        for i, v in enumerate((x, y, zz, x * x + y * y + zz * zz)):
            pay[0, 0, 24 + 4 * b + i : 25 + 4 * b + i, :] = v
    fx = fsp[0:1, :] - (base + 2.0)
    fy = fsp[1:2, :]
    for i, v in enumerate((fx, fy, fsp[2:3, :] * fsp[3:4, :], fx * fx + fy * fy)):
        pay[0, 0, 36 + i : 37 + i, :] = v

    pl.semaphore_wait(barrier, tiles + 1)

    def direct(o):
        return pltpu.make_async_remote_copy(
            src_ref=pay.at[0, 0], dst_ref=pay.at[o, 0],
            send_sem=s_dir.at[o], recv_sem=r_dir.at[o],
            device_id=(g, 2 * lax.rem(z + o, nz) + core), device_id_type=MESH,
        )

    def relay(o):
        return pltpu.make_async_remote_copy(
            src_ref=pay.at[o, 0], dst_ref=pay.at[o, 1],
            send_sem=s_rel.at[o], recv_sem=r_rel.at[o],
            device_id=(g, partner), device_id_type=MESH,
        )

    def points(i):
        return pltpu.make_async_remote_copy(
            src_ref=pay.at[0, 0, pl.ds(24, 16)], dst_ref=nbr.at[i],
            send_sem=s_nb.at[i], recv_sem=r_nb.at[i],
            device_id=((following, preceding)[i], s), device_id_type=MESH,
        )

    def give_back(i):
        return pltpu.make_async_remote_copy(
            src_ref=reto.at[i], dst_ref=reti.at[i],
            send_sem=s_ret.at[i], recv_sem=r_ret.at[i],
            device_id=((following, preceding)[i], s), device_id_type=MESH,
        )

    def forces(d, slot):
        return pltpu.make_async_remote_copy(
            src_ref=frc.at[slot], dst_ref=frc.at[slot],
            send_sem=s_f.at[d], recv_sem=r_f.at[slot],
            device_id=(g, lax.rem(s + d, tiles)), device_id_type=MESH,
        )

    def order(k):
        half = (k + 1) // 2
        return jnp.where(lax.rem(k, 2) == 1, half, lax.rem(nz - half, nz))

    points(0).start()
    points(1).start()
    relay(0).start()
    for h in range(1, nz // 2 + 1):
        direct(h).start()
        if h != nz - h:
            direct(nz - h).start()

    row_i = lax.broadcasted_iota(jnp.int32, (16, prs.shape[1]), 0)
    first = jnp.full(row_i.shape, -9, jnp.int32)
    second = first
    for r, (i, j) in enumerate(PAIRS):
        first = jnp.where(row_i == r, i, first)
        second = jnp.where(row_i == r, j, second)
    found = (prs[0:1, :] == first + 3 * g) & (prs[1:2, :] == second + 3 * g)
    hit = jnp.sum(jnp.where(found, 1.0, 0.0), axis=1, keepdims=True)
    msk[...] = jnp.broadcast_to(hit, (16, 128))

    def allowed(i, j):
        r = PAIRS.index((i, j))
        return jnp.broadcast_to(msk[r : r + 1, :], (8, 128))

    row8 = lax.broadcasted_iota(jnp.int32, (8, 128), 0)

    def put_target(ref, half, at, x, y, zz, use_z=True):
        m = x * x + y * y + zz * zz + SOFTEN
        r = jnp.where(row8 < 4, row8, row8 - 4)
        u = jnp.where(r == 0, -2.0 * x, jnp.where(r == 1, -2.0 * y, 0.0))
        if use_z:
            u = jnp.where(r == 2, -2.0 * zz, u)
        u = jnp.where(row8 == 3, 1.0, jnp.where(row8 == 7, m, u))
        u1, u2, u3 = split3(u)
        a = jnp.where((row8 < 4) | (row8 == 7), u1, u2)
        b = jnp.where(row8 == 7, u2, a)
        c = jnp.where((row8 < 3) | (row8 == 7), u3, u1)
        t = [a, b, c]
        zero = [jnp.zeros((8, 128), F32)] * 3
        t = t + zero if half == 0 else zero + t
        ref[:, 128 * at : 128 * at + 128] = jnp.concatenate(t, axis=0).astype(BF16)

    def spread(ref, r):
        return jnp.broadcast_to(ref[r : r + 1, :], (8, 128))

    def target(ref, b, at, points, r, shift):
        put_target(
            ref, b % 2, at, spread(points, r) + 2.0 * shift, spread(points, r + 1),
            spread(points, r + 2),
        )

    mine = pay.at[0, 0]
    for b in range(3):
        for t in range(2):
            target(tgt.at[b], b, 4 + t, mine, 24 + 4 * t, t - b)
        target(tgp.at[b // 2], b, b % 2, mine, 32, 2 - b)
        put_target(
            tgv.at[b // 2], b % 2, b % 2, spread(mine, 36) + 2.0 * (1 - b),
            spread(mine, 37), jnp.full((8, 128), DEPTH, F32),
        )
    for t in range(3):
        put_target(
            tgf if t < 2 else tgp.at[1], 1, t if t < 2 else 1,
            spread(mine, 24 + 4 * t) + 2.0 * (t - 1), spread(mine, 25 + 4 * t),
            spread(mine, 26 + 4 * t) - DEPTH, use_z=False,
        )

    for ref in (acc, accp, accf, accv, accw):
        ref[...] = jnp.zeros_like(ref)

    points(0).wait_recv()
    points(1).wait_recv()
    for b in range(3):
        for at, (side, t) in enumerate(CROSS[b]):
            target(tgt.at[b], b, at, nbr.at[0 if side < 0 else 1], 4 * t, 3 * side + t - b)

    row = lax.broadcasted_iota(jnp.int32, (8, 256), 0)

    def both(o, r):
        return jnp.concatenate([pay[o, 0, r : r + 8, :], pay[o, 1, r : r + 8, :]], axis=1)

    def sources(o):
        made = []
        for i, p in enumerate((both(o, 24), both(o, 32))):
            q = pltpu.roll(p, 4, 0)
            groups = []
            for lo, hi in ((p, q), (q, p)):
                e = jnp.where(row < 4, lo, jnp.where(row < 7, hi, 1.0))
                e1, e2, e3 = split3(e)
                last = row == 7
                groups += [
                    e1, jnp.where(last, 1.0, e2),
                    jnp.where((row < 3) | last, e1, e3),
                ]
            made.append(jnp.concatenate(groups, axis=0).T.astype(BF16))
            ft[o, i] = made[i]
        return made

    def sweep(features, targets, lhs, cubed=False):
        total = None
        for c in range(2):
            rows = features[128 * c : 128 * c + 128, :]
            left = lhs[:, 128 * c : 128 * c + 128]
            d2 = jnp.dot(rows, targets, preferred_element_type=F32)
            k = lax.rsqrt(d2)
            if cubed:
                k = k * k * k
            hi = k.astype(BF16)
            lo = (k - hi.astype(F32)).astype(BF16)
            part = jnp.dot(left, hi, preferred_element_type=F32)
            part += jnp.dot(left, lo, preferred_element_type=F32)
            total = part if total is None else total + part
        return total

    def main_step(j, carry):
        chips = [order(2 * j), order(2 * j + 1)]

        @pl.when(j < nz // 2 - 1)
        def _():
            for k in (2, 3):
                ahead = order(2 * j + k)
                direct(ahead).wait_recv()
                relay(ahead).start()

        for o in chips:
            relay(o).wait_recv()
        made = [sources(o) for o in chips]
        lhs = [[split2(both(o, 8 * b)) for b in range(3)] for o in chips]
        for b in range(3):
            for n in (0, 256, 512):
                block = pl.ds(n, 256)
                acc[b, :, block] += sum(
                    sweep(made[i][b // 2], tgt[b, :, block], lhs[i][b]) for i in range(2)
                )
        return carry

    direct(1).wait_recv()
    relay(1).start()
    lax.fori_loop(0, nz // 2, main_step, 0)

    def result(b, at):
        lanes = pl.ds(128 * at, 128)
        return acc[b, 0:8, lanes] + acc[b, 8:16, lanes]

    for i, side in enumerate((+1, -1)):
        for t in range(3):
            total = jnp.zeros((8, 128), F32)
            for b in range(3):
                if (side, t) in CROSS[b]:
                    pair = (b, 3 + t) if side > 0 else (t - 3, b)
                    total += result(b, CROSS[b].index((side, t))) * allowed(*pair)
            reto[i, t] = total
    give_back(0).start()
    give_back(1).start()

    def own_step(j, carry):
        first, second, third = 0.0, 0.0, 0.0
        for o in (2 * j, 2 * j + 1):
            surface = split2(both(o, 32))
            w = [split2(both(o, 8 * b)) for b in range(3)]
            first += sweep(ft[o, 0], tgp[0], jnp.concatenate([w[0], w[1]], axis=0))
            second += sweep(ft[o, 1], tgp[1], jnp.concatenate([w[2], surface], axis=0))
            third += sweep(ft[o, 1], tgf[...], surface)
        accp[0] += first
        accp[1] += second
        accf[...] += third
        return carry

    lax.fori_loop(0, nz // 2, own_step, 0)

    give_back(0).wait_recv()
    give_back(1).wait_recv()
    lane = lax.broadcasted_iota(jnp.int32, (8, 128), 1)
    packed = jnp.zeros((8, 128), F32)
    for t in range(3):
        total = reti[0, t] + reti[1, t]
        for b in range(3):
            if t < 2:
                r = result(b, 4 + t)
            else:
                top, lanes = 16 * (b % 2), pl.ds(128 * (b % 2), 128)
                r = accp[b // 2, top : top + 8, lanes] + accp[b // 2, top + 8 : top + 16, lanes]
            total += r if b == t else r * allowed(min(b, t), max(b, t))
        if t < 2:
            surface = accf[6:7, 128 * t : 128 * t + 128] + accf[14:15, 128 * t : 128 * t + 128]
        else:
            surface = accp[1, 22:23, 128:256] + accp[1, 30:31, 128:256]
        total += jnp.where(row8 == 0, surface, 0.0)
        pot[t] = total
        for k in range(3):
            an = bn[k, t : t + 1, :] * bp[3, t : t + 1, :]
            column = jnp.sum(total * an, axis=1, keepdims=True)
            packed = jnp.where(lane == 8 * (3 * t + k) + row8, column, packed)
    frc[s] = jnp.sum(packed, axis=0, keepdims=True)
    for d in range(1, tiles):
        forces(d, s).start()

    def velocity_step(j, carry):
        first, second = 0.0, 0.0
        for o in (2 * j, 2 * j + 1):
            lhs = []
            for b in range(3):
                tile = both(o, 24 if b < 2 else 32)
                w0 = jnp.broadcast_to(both(o, 8 * b)[0:1, :], (8, 256))
                lhs.append(split2(w0 * jnp.where(row == (7 if b == 1 else 3), 1.0, tile)))
            first += sweep(ft[o, 0], tgv[0], jnp.concatenate(lhs[:2], axis=0), cubed=True)
            second += sweep(ft[o, 1], tgv[1, :, 0:128], lhs[2], cubed=True)
        accv[...] += first
        accw[...] += second
        return carry

    lax.fori_loop(0, nz // 2, velocity_step, 0)

    v = [jnp.zeros((1, 128), F32)] * 3
    for b in range(3):
        ref = accv if b < 2 else accw
        top, lanes = 16 * (b % 2), pl.ds(128 * (b % 2), 128)
        moments = ref[top : top + 8, lanes] + ref[top + 8 : top + 16, lanes]
        r = 4 if b == 1 else 0
        point = (pay[0, 0, 36:37, :] + 2.0 * (1 - b), pay[0, 0, 37:38, :], DEPTH)
        for i in range(3):
            v[i] = v[i] + (moments[r + i : r + i + 1] - point[i] * moments[r + 3 : r + 4])
    speed_sq = v[0] * v[0] + v[1] * v[1] + v[2] * v[2]
    phi, eta = fst[0:1, :], fst[1:2, :]
    fsn[0:1, :] = phi + STEP * (-GRAVITY * eta - 0.5 * speed_sq)
    fsn[1:2, :] = eta + STEP * v[2]

    for d in range(1, tiles):
        forces(0, lax.rem(s + d, tiles)).wait_recv()
    whole = frc[0]
    for i in range(1, tiles):
        whole = whole + frc[i]
    for t in range(3):
        for k in range(3):
            at = 8 * (3 * t + k)
            force[t, k : k + 1, :] = whole[:, at : at + 8]

    for i in range(2):
        points(i).wait_send()
        give_back(i).wait_send()
    for o in range(nz):
        relay(o).wait_send()
        if o:
            direct(o).wait_send()
    for d in range(1, tiles):
        forces(d, s).wait_send()


def write_out(pot, force, fsn, pot_out, force_out, fsn_out):
    pot_out[...] = pot[...]
    force_out[...] = force[...]
    fsn_out[...] = fsn[...]


def on_device(bp, bn, fsp, fst, pairs):
    nz = lax.axis_size("surf") // 2
    tiles = 2 * nz
    dma = pltpu.SemaphoreType.DMA
    vmem = pl.BlockSpec(memory_space=pltpu.VMEM)
    shapes = (
        jax.ShapeDtypeStruct((3, 8, 128), F32),
        jax.ShapeDtypeStruct((3, 3, 8), F32),
        jax.ShapeDtypeStruct((2, 128), F32),
    )
    outs = pl.pallas_call(
        functools.partial(kernel, nz),
        out_shape=shapes,
        in_specs=[vmem] * 5,
        out_specs=(vmem,) * 3,
        scratch_shapes=[
            pltpu.VMEM((nz, 2, 40, 128), F32),
            pltpu.VMEM((2, 16, 128), F32),
            pltpu.VMEM((3, 48, 768), BF16),
            pltpu.VMEM((2, 48, 256), BF16),
            pltpu.VMEM((48, 256), BF16),
            pltpu.VMEM((2, 48, 256), BF16),
            pltpu.VMEM((nz, 2, 256, 48), BF16),
            pltpu.VMEM((3, 16, 768), F32),
            pltpu.VMEM((2, 32, 256), F32),
            pltpu.VMEM((16, 256), F32),
            pltpu.VMEM((32, 256), F32),
            pltpu.VMEM((16, 128), F32),
            pltpu.VMEM((2, 3, 8, 128), F32),
            pltpu.VMEM((2, 3, 8, 128), F32),
            pltpu.VMEM((16, 128), F32),
            pltpu.VMEM((tiles, 1, 128), F32),
            dma((nz,)), dma((nz,)), dma((nz,)), dma((nz,)),
            dma((2,)), dma((2,)), dma((2,)), dma((2,)),
            dma((tiles,)), dma((tiles,)),
        ],
        compiler_params=pltpu.CompilerParams(collective_id=0, has_side_effects=True),
        name="section",
    )(bp, bn, fsp, fst, pairs.T)
    pot, force, fsn = pl.pallas_call(
        write_out, out_shape=shapes, in_specs=[vmem] * 3, out_specs=(vmem,) * 3, name="write_out"
    )(*outs)
    return pot, force.transpose(0, 2, 1), fsn


def solution(mesh):
    placed = (
        P(None, "body", "surf"),
        P(None, "body", "surf"),
        P(None, ("body", "surf")),
        P(None, ("body", "surf")),
        P(),
    )
    return jax.shard_map(
        on_device,
        mesh=mesh,
        in_specs=placed,
        out_specs=(P("body", None, "surf"), P("body", None, None), P(None, ("body", "surf"))),
        check_vma=False,
    )
```

```python
import functools

import jax
import jax.numpy as jnp
from jax import lax
from jax.experimental import pallas as pl
from jax.experimental.pallas import tpu as pltpu
from jax.sharding import PartitionSpec as P

MESH = pl.DeviceIdType.MESH
F32 = jnp.float32
BF16 = jnp.bfloat16
SOFTEN = 0.01
GRAVITY = 9.81
STEP = 0.2
DEPTH = 1.5

CROSS = [
    [(+1, t) for t in range(b + 1)] + [(-1, t) for t in range(b, 3)] for b in range(3)
]
PAIRS = [(0, 1), (0, 2), (1, 2)]
PAIRS += [(b, 3 + t) for b in range(3) for t in range(b + 1)]
PAIRS += [(t - 3, b) for b in range(3) for t in range(b, 3)]


def rounded(x):
    return x.astype(BF16).astype(F32)


def split3(x):
    a = rounded(x)
    r = x - a
    b = rounded(r)
    return a, b, rounded(r - b)


def split2(x):
    a = rounded(x)
    return jnp.concatenate([a, x - a], axis=0).astype(BF16)


def kernel(
    nz,
    bp_in, bn_in, fsp_in, fst_in, prs_in,
    pot, force, fsn,
    bp, bn, fsp, fst, prs,
    pay, nbr, tgt, tgp, tgf, tgv, ft, acc, accp, accf, accv, accw, reto, reti, msk, frc,
    s_in, s_dir, r_dir, s_rel, r_rel, s_nb, r_nb, s_ret, r_ret, s_f, r_f,
):
    groups = lax.axis_size("body")
    tiles = 2 * nz
    g = lax.axis_index("body")
    s = lax.axis_index("surf")
    z, core = s // 2, lax.rem(s, 2)
    partner = 2 * z + 1 - core
    following = lax.rem(g + 1, groups)
    preceding = lax.rem(g + groups - 1, groups)

    barrier = pltpu.get_barrier_semaphore()
    for d in range(1, tiles):
        pl.semaphore_signal(
            barrier, inc=1, device_id=(g, lax.rem(s + d, tiles)), device_id_type=MESH
        )
    has_following, has_preceding = g < groups - 1, g > 0

    @pl.when(has_following)
    def _():
        pl.semaphore_signal(barrier, inc=1, device_id=(following, s), device_id_type=MESH)

    @pl.when(has_preceding)
    def _():
        pl.semaphore_signal(barrier, inc=1, device_id=(preceding, s), device_id_type=MESH)

    inputs = [
        pltpu.make_async_copy(a, b, s_in.at[i])
        for i, (a, b) in enumerate(
            ((bp_in, bp), (fsp_in, fsp), (prs_in, prs), (bn_in, bn), (fst_in, fst))
        )
    ]
    for copy in inputs:
        copy.start()

    @pl.when(g == 0)
    def _():
        nbr[0] = jnp.zeros_like(nbr[0])
        reti[0] = jnp.zeros_like(reti[0])

    @pl.when(g == groups - 1)
    def _():
        nbr[1] = jnp.zeros_like(nbr[1])
        reti[1] = jnp.zeros_like(reti[1])

    inputs[0].wait()
    inputs[1].wait()

    base = 6.0 * g.astype(F32)
    area = bp[3]
    for k in range(8):
        w = bp[4 + k] * area
        for b in range(3):
            pay[0, 0, 8 * b + k : 8 * b + k + 1, :] = w[b : b + 1, :]
    for b in range(3):
        x = bp[0, b : b + 1, :] - (base + 2.0 * b)
        y = bp[1, b : b + 1, :]
        zz = bp[2, b : b + 1, :] + DEPTH
        for i, v in enumerate((x, y, zz, x * x + y * y + zz * zz)):
            pay[0, 0, 24 + 4 * b + i : 25 + 4 * b + i, :] = v
    fx = fsp[0:1, :] - (base + 2.0)
    fy = fsp[1:2, :]
    for i, v in enumerate((fx, fy, fsp[2:3, :] * fsp[3:4, :], fx * fx + fy * fy)):
        pay[0, 0, 36 + i : 37 + i, :] = v

    pl.semaphore_wait(
        barrier,
        tiles - 1 + (g + groups - 1) // groups + (2 * groups - 2 - g) // groups,
    )

    def direct(o):
        return pltpu.make_async_remote_copy(
            src_ref=pay.at[0, 0], dst_ref=pay.at[o, 0],
            send_sem=s_dir.at[o], recv_sem=r_dir.at[o],
            device_id=(g, 2 * lax.rem(z + o, nz) + core), device_id_type=MESH,
        )

    def relay(o):
        return pltpu.make_async_remote_copy(
            src_ref=pay.at[o, 0], dst_ref=pay.at[o, 1],
            send_sem=s_rel.at[o], recv_sem=r_rel.at[o],
            device_id=(g, partner), device_id_type=MESH,
        )

    far = nz // 2

    def across():
        return pltpu.make_async_remote_copy(
            src_ref=pay.at[0, 0], dst_ref=pay.at[far, 1],
            send_sem=s_rel.at[far], recv_sem=r_rel.at[far],
            device_id=(g, 2 * lax.rem(z + far, nz) + 1 - core), device_id_type=MESH,
        )

    def points(i):
        return pltpu.make_async_remote_copy(
            src_ref=pay.at[0, 0, pl.ds(24, 16)], dst_ref=nbr.at[i],
            send_sem=s_nb.at[i], recv_sem=r_nb.at[i],
            device_id=((following, preceding)[i], s), device_id_type=MESH,
        )

    def give_back(i):
        return pltpu.make_async_remote_copy(
            src_ref=reto.at[i], dst_ref=reti.at[i],
            send_sem=s_ret.at[i], recv_sem=r_ret.at[i],
            device_id=((following, preceding)[i], s), device_id_type=MESH,
        )

    def forces(d, slot):
        return pltpu.make_async_remote_copy(
            src_ref=frc.at[slot], dst_ref=frc.at[slot],
            send_sem=s_f.at[d], recv_sem=r_f.at[slot],
            device_id=(g, lax.rem(s + d, tiles)), device_id_type=MESH,
        )

    def order(k):
        half = (k + 1) // 2
        return jnp.where(lax.rem(k, 2) == 1, half, lax.rem(nz - half, nz))

    def sides(first, second):
        pl.when(has_following)(first)
        pl.when(has_preceding)(second)

    sides(lambda: points(0).start(), lambda: points(1).start())
    relay(0).start()
    for h in range(1, nz // 2 + 1):
        direct(h).start()
        if h != nz - h:
            direct(nz - h).start()
    across().start()
    inputs[2].wait()

    row_i = lax.broadcasted_iota(jnp.int32, (16, prs.shape[1]), 0)
    first = jnp.full(row_i.shape, -9, jnp.int32)
    second = first
    for r, (i, j) in enumerate(PAIRS):
        first = jnp.where(row_i == r, i, first)
        second = jnp.where(row_i == r, j, second)
    found = (prs[0:1, :] == first + 3 * g) & (prs[1:2, :] == second + 3 * g)
    hit = jnp.sum(jnp.where(found, 1.0, 0.0), axis=1, keepdims=True)
    msk[...] = jnp.broadcast_to(hit, (16, 128))

    def allowed(i, j):
        r = PAIRS.index((i, j))
        return jnp.broadcast_to(msk[r : r + 1, :], (8, 128))

    row8 = lax.broadcasted_iota(jnp.int32, (8, 128), 0)

    def put_target(ref, half, at, x, y, zz, use_z=True):
        m = x * x + y * y + zz * zz + SOFTEN
        r = jnp.where(row8 < 4, row8, row8 - 4)
        u = jnp.where(r == 0, -2.0 * x, jnp.where(r == 1, -2.0 * y, 0.0))
        if use_z:
            u = jnp.where(r == 2, -2.0 * zz, u)
        u = jnp.where(row8 == 3, 1.0, jnp.where(row8 == 7, m, u))
        u1, u2, u3 = split3(u)
        a = jnp.where((row8 < 4) | (row8 == 7), u1, u2)
        b = jnp.where(row8 == 7, u2, a)
        c = jnp.where((row8 < 3) | (row8 == 7), u3, u1)
        t = [a, b, c]
        zero = [jnp.zeros((8, 128), F32)] * 3
        t = t + zero if half == 0 else zero + t
        ref[:, 128 * at : 128 * at + 128] = jnp.concatenate(t, axis=0).astype(BF16)

    def spread(ref, r):
        return jnp.broadcast_to(ref[r : r + 1, :], (8, 128))

    def target(ref, b, at, points, r, shift):
        put_target(
            ref, b % 2, at, spread(points, r) + 2.0 * shift, spread(points, r + 1),
            spread(points, r + 2),
        )

    mine = pay.at[0, 0]
    for b in range(3):
        for t in range(2):
            target(tgt.at[b], b, 4 + t, mine, 24 + 4 * t, t - b)
        target(tgp.at[b // 2], b, b % 2, mine, 32, 2 - b)
        put_target(
            tgv.at[b // 2], b % 2, b % 2, spread(mine, 36) + 2.0 * (1 - b),
            spread(mine, 37), jnp.full((8, 128), DEPTH, F32),
        )
    for t in range(3):
        put_target(
            tgf if t < 2 else tgp.at[1], 1, t if t < 2 else 1,
            spread(mine, 24 + 4 * t) + 2.0 * (t - 1), spread(mine, 25 + 4 * t),
            spread(mine, 26 + 4 * t) - DEPTH, use_z=False,
        )

    for ref in (acc, accp, accf, accv, accw):
        ref[...] = jnp.zeros_like(ref)

    sides(lambda: points(1).wait_recv(), lambda: points(0).wait_recv())
    for b in range(3):
        for at, (side, t) in enumerate(CROSS[b]):
            target(tgt.at[b], b, at, nbr.at[0 if side < 0 else 1], 4 * t, 3 * side + t - b)

    row = lax.broadcasted_iota(jnp.int32, (8, 256), 0)

    def both(o, r):
        return jnp.concatenate([pay[o, 0, r : r + 8, :], pay[o, 1, r : r + 8, :]], axis=1)

    def sources(o):
        made = []
        for i, p in enumerate((both(o, 24), both(o, 32))):
            q = pltpu.roll(p, 4, 0)
            groups = []
            for lo, hi in ((p, q), (q, p)):
                e = jnp.where(row < 4, lo, jnp.where(row < 7, hi, 1.0))
                e1, e2, e3 = split3(e)
                last = row == 7
                groups += [
                    e1, jnp.where(last, 1.0, e2),
                    jnp.where((row < 3) | last, e1, e3),
                ]
            made.append(jnp.concatenate(groups, axis=0).T.astype(BF16))
            ft[o, i] = made[i]
        return made

    def sweep(features, targets, lhs, cubed=False):
        total = None
        for c in range(2):
            rows = features[128 * c : 128 * c + 128, :]
            left = lhs[:, 128 * c : 128 * c + 128]
            d2 = jnp.dot(rows, targets, preferred_element_type=F32)
            k = lax.rsqrt(d2)
            if cubed:
                k = k * k * k
            hi = k.astype(BF16)
            lo = (k - hi.astype(F32)).astype(BF16)
            part = jnp.dot(left, hi, preferred_element_type=F32)
            part += jnp.dot(left, lo, preferred_element_type=F32)
            total = part if total is None else total + part
        return total

    def arrive(k):
        direct(order(k)).wait_recv()

        @pl.when(k < nz - 1)
        def _():
            relay(order(k)).start()

    def meet(chips, blocks):
        for o in chips:
            relay(o).wait_recv()
        made = [sources(o) for o in chips]
        lhs = [[split2(both(o, 8 * b)) for b in range(3)] for o in chips]
        for b in range(3):
            for n in blocks:
                block = pl.ds(n, 256)
                acc[b, :, block] += sum(
                    sweep(made[i][b // 2], tgt[b, :, block], lhs[i][b]) for i in range(2)
                )

    def main_step(j, carry):
        arrive(2 * j + 2)
        arrive(2 * j + 3)
        meet([order(2 * j), order(2 * j + 1)], (0, 256, 512))
        return carry

    arrive(1)
    lax.fori_loop(0, nz // 2 - 1, main_step, 0)
    last = [order(nz - 2), order(nz - 1)]
    meet(last, (0, 256))

    def result(b, at):
        lanes = pl.ds(128 * at, 128)
        return acc[b, 0:8, lanes] + acc[b, 8:16, lanes]

    for i, side in enumerate((+1, -1)):
        for t in range(3):
            total = jnp.zeros((8, 128), F32)
            for b in range(3):
                if (side, t) in CROSS[b]:
                    pair = (b, 3 + t) if side > 0 else (t - 3, b)
                    total += result(b, CROSS[b].index((side, t))) * allowed(*pair)
            reto[i, t] = total
    sides(lambda: give_back(0).start(), lambda: give_back(1).start())

    def own_step(j, carry):
        first, second, third = 0.0, 0.0, 0.0
        for o in (2 * j, 2 * j + 1):
            surface = split2(both(o, 32))
            w = [split2(both(o, 8 * b)) for b in range(3)]
            first += sweep(ft[o, 0], tgp[0], jnp.concatenate([w[0], w[1]], axis=0))
            second += sweep(ft[o, 1], tgp[1], jnp.concatenate([w[2], surface], axis=0))
            third += sweep(ft[o, 1], tgf[...], surface)
        accp[0] += first
        accp[1] += second
        accf[...] += third
        return carry

    lax.fori_loop(0, nz // 2, own_step, 0)
    for b in range(3):
        acc[b, :, 512:768] += sum(
            sweep(ft[o, b // 2], tgt[b, :, 512:768], split2(both(o, 8 * b))) for o in last
        )

    sides(lambda: give_back(1).wait_recv(), lambda: give_back(0).wait_recv())
    inputs[3].wait()
    lane = lax.broadcasted_iota(jnp.int32, (8, 128), 1)
    packed = jnp.zeros((8, 128), F32)
    for t in range(3):
        total = reti[0, t] + reti[1, t]
        for b in range(3):
            if t < 2:
                r = result(b, 4 + t)
            else:
                top, lanes = 16 * (b % 2), pl.ds(128 * (b % 2), 128)
                r = accp[b // 2, top : top + 8, lanes] + accp[b // 2, top + 8 : top + 16, lanes]
            total += r if b == t else r * allowed(min(b, t), max(b, t))
        if t < 2:
            surface = accf[6:7, 128 * t : 128 * t + 128] + accf[14:15, 128 * t : 128 * t + 128]
        else:
            surface = accp[1, 22:23, 128:256] + accp[1, 30:31, 128:256]
        total += jnp.where(row8 == 0, surface, 0.0)
        pot[t] = total
        for k in range(3):
            an = bn[k, t : t + 1, :] * bp[3, t : t + 1, :]
            column = jnp.sum(total * an, axis=1, keepdims=True)
            packed = jnp.where(lane == 8 * (3 * t + k) + row8, column, packed)
    frc[s] = jnp.sum(packed, axis=0, keepdims=True)
    for d in range(1, tiles):
        forces(d, s).start()

    def velocity_step(j, carry):
        first, second = 0.0, 0.0
        for o in (2 * j, 2 * j + 1):
            lhs = []
            for b in range(3):
                tile = both(o, 24 if b < 2 else 32)
                w0 = jnp.broadcast_to(both(o, 8 * b)[0:1, :], (8, 256))
                lhs.append(split2(w0 * jnp.where(row == (7 if b == 1 else 3), 1.0, tile)))
            first += sweep(ft[o, 0], tgv[0], jnp.concatenate(lhs[:2], axis=0), cubed=True)
            second += sweep(ft[o, 1], tgv[1, :, 0:128], lhs[2], cubed=True)
        accv[...] += first
        accw[...] += second
        return carry

    lax.fori_loop(0, nz // 2, velocity_step, 0)

    v = [jnp.zeros((1, 128), F32)] * 3
    for b in range(3):
        ref = accv if b < 2 else accw
        top, lanes = 16 * (b % 2), pl.ds(128 * (b % 2), 128)
        moments = ref[top : top + 8, lanes] + ref[top + 8 : top + 16, lanes]
        r = 4 if b == 1 else 0
        point = (pay[0, 0, 36:37, :] + 2.0 * (1 - b), pay[0, 0, 37:38, :], DEPTH)
        for i in range(3):
            v[i] = v[i] + (moments[r + i : r + i + 1] - point[i] * moments[r + 3 : r + 4])
    inputs[4].wait()
    speed_sq = v[0] * v[0] + v[1] * v[1] + v[2] * v[2]
    phi, eta = fst[0:1, :], fst[1:2, :]
    fsn[0:1, :] = phi + STEP * (-GRAVITY * eta - 0.5 * speed_sq)
    fsn[1:2, :] = eta + STEP * v[2]

    for d in range(1, tiles):
        forces(0, lax.rem(s + d, tiles)).wait_recv()
    whole = frc[0]
    for i in range(1, tiles):
        whole = whole + frc[i]
    for t in range(3):
        for k in range(3):
            at = 8 * (3 * t + k)
            force[t, k : k + 1, :] = whole[:, at : at + 8]

    sides(lambda: points(0).wait_send(), lambda: points(1).wait_send())
    sides(lambda: give_back(0).wait_send(), lambda: give_back(1).wait_send())
    for o in range(nz):
        (across() if o == far else relay(o)).wait_send()
        if o:
            direct(o).wait_send()
    for d in range(1, tiles):
        forces(d, s).wait_send()


def write_out(pot, force, fsn, pot_out, force_out, fsn_out):
    pot_out[...] = pot[...]
    force_out[...] = force[...]
    fsn_out[...] = fsn[...]


def on_device(bp, bn, fsp, fst, pairs):
    nz = lax.axis_size("surf") // 2
    tiles = 2 * nz
    dma = pltpu.SemaphoreType.DMA
    vmem = pl.BlockSpec(memory_space=pltpu.VMEM)
    shapes = (
        jax.ShapeDtypeStruct((3, 8, 128), F32),
        jax.ShapeDtypeStruct((3, 3, 8), F32),
        jax.ShapeDtypeStruct((2, 128), F32),
    )
    outs = pl.pallas_call(
        functools.partial(kernel, nz),
        out_shape=shapes,
        in_specs=[pl.BlockSpec(memory_space=pl.ANY)] * 5,
        out_specs=(vmem,) * 3,
        scratch_shapes=[
            pltpu.VMEM(bp.shape, F32),
            pltpu.VMEM(bn.shape, F32),
            pltpu.VMEM(fsp.shape, F32),
            pltpu.VMEM(fst.shape, F32),
            pltpu.VMEM(pairs.shape[::-1], jnp.int32),
            pltpu.VMEM((nz, 2, 40, 128), F32),
            pltpu.VMEM((2, 16, 128), F32),
            pltpu.VMEM((3, 48, 768), BF16),
            pltpu.VMEM((2, 48, 256), BF16),
            pltpu.VMEM((48, 256), BF16),
            pltpu.VMEM((2, 48, 256), BF16),
            pltpu.VMEM((nz, 2, 256, 48), BF16),
            pltpu.VMEM((3, 16, 768), F32),
            pltpu.VMEM((2, 32, 256), F32),
            pltpu.VMEM((16, 256), F32),
            pltpu.VMEM((32, 256), F32),
            pltpu.VMEM((16, 128), F32),
            pltpu.VMEM((2, 3, 8, 128), F32),
            pltpu.VMEM((2, 3, 8, 128), F32),
            pltpu.VMEM((16, 128), F32),
            pltpu.VMEM((tiles, 1, 128), F32),
            dma((5,)), dma((nz,)), dma((nz,)), dma((nz,)), dma((nz,)),
            dma((2,)), dma((2,)), dma((2,)), dma((2,)),
            dma((tiles,)), dma((tiles,)),
        ],
        compiler_params=pltpu.CompilerParams(collective_id=0, has_side_effects=True),
        name="section",
    )(bp, bn, fsp, fst, pairs.T)
    pot, force, fsn = pl.pallas_call(
        write_out, out_shape=shapes, in_specs=[vmem] * 3, out_specs=(vmem,) * 3, name="write_out"
    )(*outs)
    return pot, force.transpose(0, 2, 1), fsn


def solution(mesh):
    placed = (
        P(None, "body", "surf"),
        P(None, "body", "surf"),
        P(None, ("body", "surf")),
        P(None, ("body", "surf")),
        P(),
    )
    return jax.shard_map(
        on_device,
        mesh=mesh,
        in_specs=placed,
        out_specs=(P("body", None, "surf"), P("body", None, None), P(None, ("body", "surf"))),
        check_vma=False,
    )
```

```python
import functools

import jax
import jax.numpy as jnp
from jax import lax
from jax.experimental import pallas as pl
from jax.experimental.pallas import tpu as pltpu
from jax.sharding import PartitionSpec as P

MESH = pl.DeviceIdType.MESH
F32 = jnp.float32
BF16 = jnp.bfloat16
SOFTEN = 0.01
GRAVITY = 9.81
STEP = 0.2
DEPTH = 1.5

CROSS = [
    [(+1, t) for t in range(b + 1)] + [(-1, t) for t in range(b, 3)] for b in range(3)
]
PAIRS = [(0, 1), (0, 2), (1, 2)]
PAIRS += [(b, 3 + t) for b in range(3) for t in range(b + 1)]
PAIRS += [(t - 3, b) for b in range(3) for t in range(b, 3)]


def rounded(x):
    return x.astype(BF16).astype(F32)


def split3(x):
    a = rounded(x)
    r = x - a
    b = rounded(r)
    return a, b, rounded(r - b)


def split2(x):
    a = rounded(x)
    return jnp.concatenate([a, x - a], axis=0).astype(BF16)


def kernel(
    nz,
    bp_in, bn_in, fsp_in, fst_in, prs_in,
    pot, force, fsn,
    bp, bn, fsp, fst, prs,
    pay, nbr, tgt, tgp, tgf, tgv, ft, acc, accp, accf, accv, accw, reto, reti, msk, frc,
    s_in, s_dir, r_dir, s_rel, r_rel, s_nb, r_nb, s_ret, r_ret, s_f, r_f,
):
    groups = lax.axis_size("body")
    tiles = 2 * nz
    g = lax.axis_index("body")
    s = lax.axis_index("surf")
    z, core = s // 2, lax.rem(s, 2)
    partner = 2 * z + 1 - core
    following = lax.rem(g + 1, groups)
    preceding = lax.rem(g + groups - 1, groups)

    barrier = pltpu.get_barrier_semaphore()
    for d in range(1, tiles):
        pl.semaphore_signal(
            barrier, inc=1, device_id=(g, lax.rem(s + d, tiles)), device_id_type=MESH
        )
    has_following, has_preceding = g < groups - 1, g > 0

    @pl.when(has_following)
    def _():
        pl.semaphore_signal(barrier, inc=1, device_id=(following, s), device_id_type=MESH)

    @pl.when(has_preceding)
    def _():
        pl.semaphore_signal(barrier, inc=1, device_id=(preceding, s), device_id_type=MESH)

    inputs = [
        pltpu.make_async_copy(a, b, s_in.at[i])
        for i, (a, b) in enumerate(
            ((bp_in, bp), (fsp_in, fsp), (prs_in, prs), (bn_in, bn), (fst_in, fst))
        )
    ]
    for copy in inputs:
        copy.start()

    @pl.when(g == 0)
    def _():
        nbr[0] = jnp.zeros_like(nbr[0])
        reti[0] = jnp.zeros_like(reti[0])

    @pl.when(g == groups - 1)
    def _():
        nbr[1] = jnp.zeros_like(nbr[1])
        reti[1] = jnp.zeros_like(reti[1])

    inputs[0].wait()
    inputs[1].wait()

    base = 6.0 * g.astype(F32)
    area = bp[3]
    for k in range(8):
        w = bp[4 + k] * area
        for b in range(3):
            pay[0, 0, 8 * b + k : 8 * b + k + 1, :] = w[b : b + 1, :]
    for b in range(3):
        x = bp[0, b : b + 1, :] - (base + 2.0 * b)
        y = bp[1, b : b + 1, :]
        zz = bp[2, b : b + 1, :] + DEPTH
        for i, v in enumerate((x, y, zz, x * x + y * y + zz * zz)):
            pay[0, 0, 24 + 4 * b + i : 25 + 4 * b + i, :] = v
    fx = fsp[0:1, :] - (base + 2.0)
    fy = fsp[1:2, :]
    for i, v in enumerate((fx, fy, fsp[2:3, :] * fsp[3:4, :], fx * fx + fy * fy)):
        pay[0, 0, 36 + i : 37 + i, :] = v

    pl.semaphore_wait(
        barrier,
        tiles - 1 + (g + groups - 1) // groups + (2 * groups - 2 - g) // groups,
    )

    def direct(o):
        return pltpu.make_async_remote_copy(
            src_ref=pay.at[0, 0], dst_ref=pay.at[o, 0],
            send_sem=s_dir.at[o], recv_sem=r_dir.at[o],
            device_id=(g, 2 * lax.rem(z + o, nz) + core), device_id_type=MESH,
        )

    def relay(o):
        return pltpu.make_async_remote_copy(
            src_ref=pay.at[o, 0], dst_ref=pay.at[o, 1],
            send_sem=s_rel.at[o], recv_sem=r_rel.at[o],
            device_id=(g, partner), device_id_type=MESH,
        )

    far = nz // 2

    def across():
        return pltpu.make_async_remote_copy(
            src_ref=pay.at[0, 0], dst_ref=pay.at[far, 1],
            send_sem=s_rel.at[far], recv_sem=r_rel.at[far],
            device_id=(g, 2 * lax.rem(z + far, nz) + 1 - core), device_id_type=MESH,
        )

    def points(i):
        return pltpu.make_async_remote_copy(
            src_ref=pay.at[0, 0, pl.ds(24, 16)], dst_ref=nbr.at[i],
            send_sem=s_nb.at[i], recv_sem=r_nb.at[i],
            device_id=((following, preceding)[i], s), device_id_type=MESH,
        )

    def give_back(i):
        return pltpu.make_async_remote_copy(
            src_ref=reto.at[i], dst_ref=reti.at[i],
            send_sem=s_ret.at[i], recv_sem=r_ret.at[i],
            device_id=((following, preceding)[i], s), device_id_type=MESH,
        )

    def forces(d, slot):
        return pltpu.make_async_remote_copy(
            src_ref=frc.at[slot], dst_ref=frc.at[slot],
            send_sem=s_f.at[d], recv_sem=r_f.at[slot],
            device_id=(g, lax.rem(s + d, tiles)), device_id_type=MESH,
        )

    def order(k):
        half = (k + 1) // 2
        return jnp.where(lax.rem(k, 2) == 1, half, lax.rem(nz - half, nz))

    def sides(first, second):
        pl.when(has_following)(first)
        pl.when(has_preceding)(second)

    sides(lambda: points(0).start(), lambda: points(1).start())
    relay(0).start()
    for h in range(1, nz // 2 + 1):
        direct(h).start()
        if h != nz - h:
            direct(nz - h).start()
    across().start()
    inputs[2].wait()

    row_i = lax.broadcasted_iota(jnp.int32, (16, prs.shape[1]), 0)
    first = jnp.full(row_i.shape, -9, jnp.int32)
    second = first
    for r, (i, j) in enumerate(PAIRS):
        first = jnp.where(row_i == r, i, first)
        second = jnp.where(row_i == r, j, second)
    found = (prs[0:1, :] == first + 3 * g) & (prs[1:2, :] == second + 3 * g)
    hit = jnp.sum(jnp.where(found, 1.0, 0.0), axis=1, keepdims=True)
    msk[...] = jnp.broadcast_to(hit, (16, 128))

    def allowed(i, j):
        r = PAIRS.index((i, j))
        return jnp.broadcast_to(msk[r : r + 1, :], (8, 128))

    row8 = lax.broadcasted_iota(jnp.int32, (8, 128), 0)

    def put_target(ref, half, at, x, y, zz, use_z=True):
        m = x * x + y * y + zz * zz + SOFTEN
        r = jnp.where(row8 < 4, row8, row8 - 4)
        u = jnp.where(r == 0, -2.0 * x, jnp.where(r == 1, -2.0 * y, 0.0))
        if use_z:
            u = jnp.where(r == 2, -2.0 * zz, u)
        u = jnp.where(row8 == 3, 1.0, jnp.where(row8 == 7, m, u))
        u1, u2, u3 = split3(u)
        a = jnp.where((row8 < 4) | (row8 == 7), u1, u2)
        b = jnp.where(row8 == 7, u2, a)
        c = jnp.where((row8 < 3) | (row8 == 7), u3, u1)
        t = [a, b, c]
        zero = [jnp.zeros((8, 128), F32)] * 3
        t = t + zero if half == 0 else zero + t
        ref[:, 128 * at : 128 * at + 128] = jnp.concatenate(t, axis=0).astype(BF16)

    def spread(ref, r):
        return jnp.broadcast_to(ref[r : r + 1, :], (8, 128))

    def target(ref, b, at, points, r, shift):
        put_target(
            ref, b % 2, at, spread(points, r) + 2.0 * shift, spread(points, r + 1),
            spread(points, r + 2),
        )

    mine = pay.at[0, 0]
    for b in range(3):
        for t in range(2):
            target(tgt.at[b], b, 4 + t, mine, 24 + 4 * t, t - b)
        target(tgp.at[b // 2], b, b % 2, mine, 32, 2 - b)
        put_target(
            tgv.at[b // 2], b % 2, b % 2, spread(mine, 36) + 2.0 * (1 - b),
            spread(mine, 37), jnp.full((8, 128), DEPTH, F32),
        )
    for t in range(3):
        put_target(
            tgf if t < 2 else tgp.at[1], 1, t if t < 2 else 1,
            spread(mine, 24 + 4 * t) + 2.0 * (t - 1), spread(mine, 25 + 4 * t),
            spread(mine, 26 + 4 * t) - DEPTH, use_z=False,
        )

    for ref in (acc, accp, accf, accv, accw):
        ref[...] = jnp.zeros_like(ref)

    row = lax.broadcasted_iota(jnp.int32, (8, 256), 0)

    def both(o, r):
        return jnp.concatenate([pay[o, 0, r : r + 8, :], pay[o, 1, r : r + 8, :]], axis=1)

    def sources(o):
        made = []
        for i, p in enumerate((both(o, 24), both(o, 32))):
            q = pltpu.roll(p, 4, 0)
            groups = []
            for lo, hi in ((p, q), (q, p)):
                e = jnp.where(row < 4, lo, jnp.where(row < 7, hi, 1.0))
                e1, e2, e3 = split3(e)
                last = row == 7
                groups += [
                    e1, jnp.where(last, 1.0, e2),
                    jnp.where((row < 3) | last, e1, e3),
                ]
            made.append(jnp.concatenate(groups, axis=0).T.astype(BF16))
            ft[o, i] = made[i]
        return made

    def sweep(features, targets, lhs, cubed=False):
        his, los = [], []
        for c in range(2):
            d2 = jnp.dot(features[128 * c : 128 * c + 128, :], targets, preferred_element_type=F32)
            k = lax.rsqrt(d2)
            if cubed:
                k = k * k * k
            hi = k.astype(BF16)
            his.append(hi)
            los.append((k - hi.astype(F32)).astype(BF16))
        part = jnp.dot(lhs, jnp.concatenate(his, axis=0), preferred_element_type=F32)
        return part + jnp.dot(lhs, jnp.concatenate(los, axis=0), preferred_element_type=F32)

    def arrive(k):
        @pl.when(k < nz)
        def _():
            direct(order(k)).wait_recv()

        @pl.when(k < nz - 1)
        def _():
            relay(order(k)).start()

    def weights(o):
        return [split2(both(o, 8 * b)) for b in range(3)]

    def meet(made, lhs, blocks):
        for b in range(3):
            for n in blocks:
                block = pl.ds(n, 256)
                acc[b, :, block] += sum(
                    sweep(f[b // 2], tgt[b, :, block], w[b]) for f, w in zip(made, lhs)
                )

    def meet_rest(chips, made):
        first, second, third = 0.0, 0.0, 0.0
        for o, f in zip(chips, made):
            surface = split2(both(o, 32))
            w = weights(o)
            first += sweep(f[0], tgp[0], jnp.concatenate([w[0], w[1]], axis=0))
            second += sweep(f[1], tgp[1], jnp.concatenate([w[2], surface], axis=0))
            third += sweep(f[1], tgf[...], surface)
        accp[0] += first
        accp[1] += second
        accf[...] += third

    def main_step(j, carry):
        arrive(2 * j + 3)
        arrive(2 * j + 4)
        chips = [order(2 * j + 1), order(2 * j + 2)]
        for o in chips:
            relay(o).wait_recv()
        meet([sources(o) for o in chips], [weights(o) for o in chips], (0, 256, 512))
        return carry

    relay(0).wait_recv()
    made = sources(0)
    meet([made], [weights(0)], (512,))
    meet_rest([0], [made])
    arrive(1)
    sides(lambda: points(1).wait_recv(), lambda: points(0).wait_recv())
    for b in range(3):
        for at, (side, t) in enumerate(CROSS[b]):
            target(tgt.at[b], b, at, nbr.at[0 if side < 0 else 1], 4 * t, 3 * side + t - b)

    meet([[ft[0, 0], ft[0, 1]]], [weights(0)], (0, 256))
    arrive(2)
    lax.fori_loop(0, nz // 2 - 1, main_step, 0)
    relay(far).wait_recv()
    meet([sources(far)], [weights(far)], (0, 256))

    def result(b, at):
        lanes = pl.ds(128 * at, 128)
        return acc[b, 0:8, lanes] + acc[b, 8:16, lanes]

    for i, side in enumerate((+1, -1)):
        for t in range(3):
            total = jnp.zeros((8, 128), F32)
            for b in range(3):
                if (side, t) in CROSS[b]:
                    pair = (b, 3 + t) if side > 0 else (t - 3, b)
                    total += result(b, CROSS[b].index((side, t))) * allowed(*pair)
            reto[i, t] = total
    sides(lambda: give_back(0).start(), lambda: give_back(1).start())

    def own_step(j, carry):
        chips = [order(2 * j + 1), order(2 * j + 2)]
        meet_rest(chips, [[ft[o, 0], ft[o, 1]] for o in chips])
        return carry

    lax.fori_loop(0, nz // 2 - 1, own_step, 0)
    made = [ft[far, 0], ft[far, 1]]
    meet([made], [weights(far)], (512,))
    meet_rest([far], [made])

    sides(lambda: give_back(1).wait_recv(), lambda: give_back(0).wait_recv())
    inputs[3].wait()
    lane = lax.broadcasted_iota(jnp.int32, (8, 128), 1)
    packed = jnp.zeros((8, 128), F32)
    for t in range(3):
        total = reti[0, t] + reti[1, t]
        for b in range(3):
            if t < 2:
                r = result(b, 4 + t)
            else:
                top, lanes = 16 * (b % 2), pl.ds(128 * (b % 2), 128)
                r = accp[b // 2, top : top + 8, lanes] + accp[b // 2, top + 8 : top + 16, lanes]
            total += r if b == t else r * allowed(min(b, t), max(b, t))
        if t < 2:
            surface = accf[6:7, 128 * t : 128 * t + 128] + accf[14:15, 128 * t : 128 * t + 128]
        else:
            surface = accp[1, 22:23, 128:256] + accp[1, 30:31, 128:256]
        total += jnp.where(row8 == 0, surface, 0.0)
        pot[t] = total
        for k in range(3):
            an = bn[k, t : t + 1, :] * bp[3, t : t + 1, :]
            column = jnp.sum(total * an, axis=1, keepdims=True)
            packed = jnp.where(lane == 8 * (3 * t + k) + row8, column, packed)
    frc[s] = jnp.sum(packed, axis=0, keepdims=True)
    for d in range(1, tiles):
        forces(d, s).start()

    def velocity_step(j, carry):
        first, second = 0.0, 0.0
        for o in (2 * j, 2 * j + 1):
            lhs = []
            for b in range(3):
                tile = both(o, 24 if b < 2 else 32)
                w0 = jnp.broadcast_to(both(o, 8 * b)[0:1, :], (8, 256))
                lhs.append(split2(w0 * jnp.where(row == (7 if b == 1 else 3), 1.0, tile)))
            first += sweep(ft[o, 0], tgv[0], jnp.concatenate(lhs[:2], axis=0), cubed=True)
            second += sweep(ft[o, 1], tgv[1, :, 0:128], lhs[2], cubed=True)
        accv[...] += first
        accw[...] += second
        return carry

    lax.fori_loop(0, nz // 2, velocity_step, 0)

    v = [jnp.zeros((1, 128), F32)] * 3
    for b in range(3):
        ref = accv if b < 2 else accw
        top, lanes = 16 * (b % 2), pl.ds(128 * (b % 2), 128)
        moments = ref[top : top + 8, lanes] + ref[top + 8 : top + 16, lanes]
        r = 4 if b == 1 else 0
        point = (pay[0, 0, 36:37, :] + 2.0 * (1 - b), pay[0, 0, 37:38, :], DEPTH)
        for i in range(3):
            v[i] = v[i] + (moments[r + i : r + i + 1] - point[i] * moments[r + 3 : r + 4])
    inputs[4].wait()
    speed_sq = v[0] * v[0] + v[1] * v[1] + v[2] * v[2]
    phi, eta = fst[0:1, :], fst[1:2, :]
    fsn[0:1, :] = phi + STEP * (-GRAVITY * eta - 0.5 * speed_sq)
    fsn[1:2, :] = eta + STEP * v[2]

    for d in range(1, tiles):
        forces(0, lax.rem(s + d, tiles)).wait_recv()
    whole = frc[0]
    for i in range(1, tiles):
        whole = whole + frc[i]
    for t in range(3):
        for k in range(3):
            at = 8 * (3 * t + k)
            force[t, k : k + 1, :] = whole[:, at : at + 8]

    sides(lambda: points(0).wait_send(), lambda: points(1).wait_send())
    sides(lambda: give_back(0).wait_send(), lambda: give_back(1).wait_send())
    for o in range(nz):
        (across() if o == far else relay(o)).wait_send()
        if o:
            direct(o).wait_send()
    for d in range(1, tiles):
        forces(d, s).wait_send()


def write_out(pot, force, fsn, pot_out, force_out, fsn_out):
    pot_out[...] = pot[...]
    force_out[...] = force[...]
    fsn_out[...] = fsn[...]


def on_device(bp, bn, fsp, fst, pairs):
    nz = lax.axis_size("surf") // 2
    tiles = 2 * nz
    dma = pltpu.SemaphoreType.DMA
    vmem = pl.BlockSpec(memory_space=pltpu.VMEM)
    shapes = (
        jax.ShapeDtypeStruct((3, 8, 128), F32),
        jax.ShapeDtypeStruct((3, 3, 8), F32),
        jax.ShapeDtypeStruct((2, 128), F32),
    )
    outs = pl.pallas_call(
        functools.partial(kernel, nz),
        out_shape=tuple(pltpu.VMEM(a.shape, a.dtype) for a in shapes),
        in_specs=[pl.BlockSpec(memory_space=pl.ANY)] * 5,
        out_specs=(vmem,) * 3,
        scratch_shapes=[
            pltpu.VMEM(bp.shape, F32),
            pltpu.VMEM(bn.shape, F32),
            pltpu.VMEM(fsp.shape, F32),
            pltpu.VMEM(fst.shape, F32),
            pltpu.VMEM(pairs.shape[::-1], jnp.int32),
            pltpu.VMEM((nz, 2, 40, 128), F32),
            pltpu.VMEM((2, 16, 128), F32),
            pltpu.VMEM((3, 48, 768), BF16),
            pltpu.VMEM((2, 48, 256), BF16),
            pltpu.VMEM((48, 256), BF16),
            pltpu.VMEM((2, 48, 256), BF16),
            pltpu.VMEM((nz, 2, 256, 48), BF16),
            pltpu.VMEM((3, 16, 768), F32),
            pltpu.VMEM((2, 32, 256), F32),
            pltpu.VMEM((16, 256), F32),
            pltpu.VMEM((32, 256), F32),
            pltpu.VMEM((16, 128), F32),
            pltpu.VMEM((2, 3, 8, 128), F32),
            pltpu.VMEM((2, 3, 8, 128), F32),
            pltpu.VMEM((16, 128), F32),
            pltpu.VMEM((tiles, 1, 128), F32),
            dma((5,)), dma((nz,)), dma((nz,)), dma((nz,)), dma((nz,)),
            dma((2,)), dma((2,)), dma((2,)), dma((2,)),
            dma((tiles,)), dma((tiles,)),
        ],
        compiler_params=pltpu.CompilerParams(collective_id=0, has_side_effects=True),
        name="section",
    )(bp, bn, fsp, fst, pairs.T)
    outs = [pltpu.with_memory_space_constraint(a, pltpu.VMEM) for a in outs]
    pot, force, fsn = pl.pallas_call(
        write_out, out_shape=shapes, in_specs=[vmem] * 3, out_specs=(vmem,) * 3, name="write_out"
    )(*outs)
    return pot, force.transpose(0, 2, 1), fsn


def solution(mesh):
    placed = (
        P(None, "body", "surf"),
        P(None, "body", "surf"),
        P(None, ("body", "surf")),
        P(None, ("body", "surf")),
        P(),
    )
    return jax.shard_map(
        on_device,
        mesh=mesh,
        in_specs=placed,
        out_specs=(P("body", None, "surf"), P("body", None, None), P(None, ("body", "surf"))),
        check_vma=False,
    )
```

```python
import functools

import jax
import jax.numpy as jnp
from jax import lax
from jax.experimental import pallas as pl
from jax.experimental.pallas import tpu as pltpu
from jax.sharding import PartitionSpec as P

MESH = pl.DeviceIdType.MESH
F32 = jnp.float32
BF16 = jnp.bfloat16
SOFTEN = 0.01
GRAVITY = 9.81
STEP = 0.2
DEPTH = 1.5

CROSS = [
    [(+1, t) for t in range(b + 1)] + [(-1, t) for t in range(b, 3)] for b in range(3)
]
PAIRS = [(0, 1), (0, 2), (1, 2)]
PAIRS += [(b, 3 + t) for b in range(3) for t in range(b + 1)]
PAIRS += [(t - 3, b) for b in range(3) for t in range(b, 3)]


def rounded(x):
    return x.astype(BF16).astype(F32)


def split3(x):
    a = rounded(x)
    r = x - a
    b = rounded(r)
    return a, b, rounded(r - b)


def split2(x):
    a = rounded(x)
    return jnp.concatenate([a, x - a], axis=0).astype(BF16)


def kernel(
    nz,
    bp_in, bn_in, fsp_in, fst_in, prs_in,
    pot, force, fsn,
    bp, bn, fsp, fst, prs,
    pay, nbr, tgt, tgp, tgf, tgv, ft, acc, accp, accf, accv, accw, reto, reti, msk, frc,
    s_in, s_dir, r_dir, s_rel, r_rel, s_nb, r_nb, s_ret, r_ret, s_f, r_f,
):
    groups = lax.axis_size("body")
    tiles = 2 * nz
    g = lax.axis_index("body")
    s = lax.axis_index("surf")
    z, core = s // 2, lax.rem(s, 2)
    partner = 2 * z + 1 - core
    following = lax.rem(g + 1, groups)
    preceding = lax.rem(g + groups - 1, groups)

    barrier = pltpu.get_barrier_semaphore()
    for d in range(1, tiles):
        pl.semaphore_signal(
            barrier, inc=1, device_id=(g, lax.rem(s + d, tiles)), device_id_type=MESH
        )
    has_following, has_preceding = g < groups - 1, g > 0

    @pl.when(has_following)
    def _():
        pl.semaphore_signal(barrier, inc=1, device_id=(following, s), device_id_type=MESH)

    @pl.when(has_preceding)
    def _():
        pl.semaphore_signal(barrier, inc=1, device_id=(preceding, s), device_id_type=MESH)

    inputs = [
        pltpu.make_async_copy(a, b, s_in.at[i])
        for i, (a, b) in enumerate(
            ((bp_in, bp), (fsp_in, fsp), (prs_in, prs), (bn_in, bn), (fst_in, fst))
        )
    ]
    for copy in inputs:
        copy.start()

    @pl.when(g == 0)
    def _():
        nbr[0] = jnp.zeros_like(nbr[0])
        reti[0] = jnp.zeros_like(reti[0])

    @pl.when(g == groups - 1)
    def _():
        nbr[1] = jnp.zeros_like(nbr[1])
        reti[1] = jnp.zeros_like(reti[1])

    inputs[0].wait()
    inputs[1].wait()

    base = 6.0 * g.astype(F32)
    area = bp[3]
    for k in range(8):
        w = bp[4 + k] * area
        for b in range(3):
            pay[0, 0, 8 * b + k : 8 * b + k + 1, :] = w[b : b + 1, :]
    for b in range(3):
        x = bp[0, b : b + 1, :] - (base + 2.0 * b)
        y = bp[1, b : b + 1, :]
        zz = bp[2, b : b + 1, :] + DEPTH
        for i, v in enumerate((x, y, zz, x * x + y * y + zz * zz)):
            pay[0, 0, 24 + 4 * b + i : 25 + 4 * b + i, :] = v
    fx = fsp[0:1, :] - (base + 2.0)
    fy = fsp[1:2, :]
    for i, v in enumerate((fx, fy, fsp[2:3, :] * fsp[3:4, :], fx * fx + fy * fy)):
        pay[0, 0, 36 + i : 37 + i, :] = v

    pl.semaphore_wait(
        barrier,
        tiles - 1 + (g + groups - 1) // groups + (2 * groups - 2 - g) // groups,
    )

    def direct(o):
        return pltpu.make_async_remote_copy(
            src_ref=pay.at[0, 0], dst_ref=pay.at[o, 0],
            send_sem=s_dir.at[o], recv_sem=r_dir.at[o],
            device_id=(g, 2 * lax.rem(z + o, nz) + core), device_id_type=MESH,
        )

    def relay(o):
        return pltpu.make_async_remote_copy(
            src_ref=pay.at[o, 0], dst_ref=pay.at[o, 1],
            send_sem=s_rel.at[o], recv_sem=r_rel.at[o],
            device_id=(g, partner), device_id_type=MESH,
        )

    far = nz // 2

    def across():
        return pltpu.make_async_remote_copy(
            src_ref=pay.at[0, 0], dst_ref=pay.at[far, 1],
            send_sem=s_rel.at[far], recv_sem=r_rel.at[far],
            device_id=(g, 2 * lax.rem(z + far, nz) + 1 - core), device_id_type=MESH,
        )

    def points(i):
        return pltpu.make_async_remote_copy(
            src_ref=pay.at[0, 0, pl.ds(24, 16)], dst_ref=nbr.at[i],
            send_sem=s_nb.at[i], recv_sem=r_nb.at[i],
            device_id=((following, preceding)[i], s), device_id_type=MESH,
        )

    def give_back(i):
        return pltpu.make_async_remote_copy(
            src_ref=reto.at[i], dst_ref=reti.at[i],
            send_sem=s_ret.at[i], recv_sem=r_ret.at[i],
            device_id=((following, preceding)[i], s), device_id_type=MESH,
        )

    def forces(d, slot):
        return pltpu.make_async_remote_copy(
            src_ref=frc.at[slot], dst_ref=frc.at[slot],
            send_sem=s_f.at[d], recv_sem=r_f.at[slot],
            device_id=(g, lax.rem(s + d, tiles)), device_id_type=MESH,
        )

    def order(k):
        half = (k + 1) // 2
        return jnp.where(lax.rem(k, 2) == 1, half, lax.rem(nz - half, nz))

    def sides(first, second):
        pl.when(has_following)(first)
        pl.when(has_preceding)(second)

    sides(lambda: points(0).start(), lambda: points(1).start())
    relay(0).start()
    for h in range(1, nz // 2 + 1):
        direct(h).start()
        if h != nz - h:
            direct(nz - h).start()
    inputs[2].wait()

    row_i = lax.broadcasted_iota(jnp.int32, (16, prs.shape[1]), 0)
    first = jnp.full(row_i.shape, -9, jnp.int32)
    second = first
    for r, (i, j) in enumerate(PAIRS):
        first = jnp.where(row_i == r, i, first)
        second = jnp.where(row_i == r, j, second)
    found = (prs[0:1, :] == first + 3 * g) & (prs[1:2, :] == second + 3 * g)
    hit = jnp.sum(jnp.where(found, 1.0, 0.0), axis=1, keepdims=True)
    msk[...] = jnp.broadcast_to(hit, (16, 128))

    def allowed(i, j):
        r = PAIRS.index((i, j))
        return jnp.broadcast_to(msk[r : r + 1, :], (8, 128))

    row8 = lax.broadcasted_iota(jnp.int32, (8, 128), 0)

    def put_target(ref, half, at, x, y, zz, use_z=True):
        m = x * x + y * y + zz * zz + SOFTEN
        r = jnp.where(row8 < 4, row8, row8 - 4)
        u = jnp.where(r == 0, -2.0 * x, jnp.where(r == 1, -2.0 * y, 0.0))
        if use_z:
            u = jnp.where(r == 2, -2.0 * zz, u)
        u = jnp.where(row8 == 3, 1.0, jnp.where(row8 == 7, m, u))
        u1, u2, u3 = split3(u)
        a = jnp.where((row8 < 4) | (row8 == 7), u1, u2)
        b = jnp.where(row8 == 7, u2, a)
        c = jnp.where((row8 < 3) | (row8 == 7), u3, u1)
        t = [a, b, c]
        zero = [jnp.zeros((8, 128), F32)] * 3
        t = t + zero if half == 0 else zero + t
        ref[:, 128 * at : 128 * at + 128] = jnp.concatenate(t, axis=0).astype(BF16)

    def spread(ref, r):
        return jnp.broadcast_to(ref[r : r + 1, :], (8, 128))

    def target(ref, b, at, points, r, shift):
        put_target(
            ref, b % 2, at, spread(points, r) + 2.0 * shift, spread(points, r + 1),
            spread(points, r + 2),
        )

    mine = pay.at[0, 0]
    for b in range(3):
        for t in range(2):
            target(tgt.at[b], b, 4 + t, mine, 24 + 4 * t, t - b)
        target(tgp.at[b // 2], b, b % 2, mine, 32, 2 - b)
        put_target(
            tgv.at[b // 2], b % 2, b % 2, spread(mine, 36) + 2.0 * (1 - b),
            spread(mine, 37), jnp.full((8, 128), DEPTH, F32),
        )
    for t in range(3):
        put_target(
            tgf if t < 2 else tgp.at[1], 1, t if t < 2 else 1,
            spread(mine, 24 + 4 * t) + 2.0 * (t - 1), spread(mine, 25 + 4 * t),
            spread(mine, 26 + 4 * t) - DEPTH, use_z=False,
        )

    for ref in (acc, accp, accf, accv, accw):
        ref[...] = jnp.zeros_like(ref)

    row = lax.broadcasted_iota(jnp.int32, (8, 256), 0)

    def both(o, r):
        return jnp.concatenate([pay[o, 0, r : r + 8, :], pay[o, 1, r : r + 8, :]], axis=1)

    def sources(o):
        made = []
        for i, p in enumerate((both(o, 24), both(o, 32))):
            q = pltpu.roll(p, 4, 0)
            groups = []
            for lo, hi in ((p, q), (q, p)):
                e = jnp.where(row < 4, lo, jnp.where(row < 7, hi, 1.0))
                e1, e2, e3 = split3(e)
                last = row == 7
                groups += [
                    e1, jnp.where(last, 1.0, e2),
                    jnp.where((row < 3) | last, e1, e3),
                ]
            made.append(jnp.concatenate(groups, axis=0).T.astype(BF16))
            ft[o, i] = made[i]
        return made

    def sweep(features, targets, lhs, cubed=False):
        his, los = [], []
        for c in range(2):
            d2 = jnp.dot(features[128 * c : 128 * c + 128, :], targets, preferred_element_type=F32)
            k = lax.rsqrt(d2)
            if cubed:
                k = k * k * k
            hi = k.astype(BF16)
            his.append(hi)
            los.append((k - hi.astype(F32)).astype(BF16))
        part = jnp.dot(lhs, jnp.concatenate(his, axis=0), preferred_element_type=F32)
        return part + jnp.dot(lhs, jnp.concatenate(los, axis=0), preferred_element_type=F32)

    def arrive(k):
        @pl.when(k < nz)
        def _():
            direct(order(k)).wait_recv()

        @pl.when(k < nz)
        def _():
            relay(order(k)).start()

    def weights(o):
        return [split2(both(o, 8 * b)) for b in range(3)]

    def meet(made, lhs, blocks, bodies=(0, 1, 2)):
        for b in bodies:
            for n in blocks:
                block = pl.ds(n, 256)
                acc[b, :, block] += sum(
                    sweep(f[b // 2], tgt[b, :, block], w[b]) for f, w in zip(made, lhs)
                )

    def meet_rest(chips, made):
        first, second, third = 0.0, 0.0, 0.0
        for o, f in zip(chips, made):
            surface = split2(both(o, 32))
            w = weights(o)
            first += sweep(f[0], tgp[0], jnp.concatenate([w[0], w[1]], axis=0))
            second += sweep(f[1], tgp[1], jnp.concatenate([w[2], surface], axis=0))
            third += sweep(f[1], tgf[...], surface)
        accp[0] += first
        accp[1] += second
        accf[...] += third

    def main_step(j, carry):
        arrive(2 * j + 3)
        arrive(2 * j + 4)
        chips = [order(2 * j + 1), order(2 * j + 2)]
        for o in chips:
            relay(o).wait_recv()
        meet([sources(o) for o in chips], [weights(o) for o in chips], (0, 256))
        return carry

    relay(0).wait_recv()
    made = sources(0)
    arrive(1)
    sides(lambda: points(1).wait_recv(), lambda: points(0).wait_recv())
    for b in range(3):
        for at, (side, t) in enumerate(CROSS[b]):
            target(tgt.at[b], b, at, nbr.at[0 if side < 0 else 1], 4 * t, 3 * side + t - b)

    meet([[ft[0, 0], ft[0, 1]]], [weights(0)], (0, 256))
    arrive(2)
    lax.fori_loop(0, nz // 2 - 1, main_step, 0)
    def result(b, at):
        lanes = pl.ds(128 * at, 128)
        return acc[b, 0:8, lanes] + acc[b, 8:16, lanes]

    def give(i, side):
        for t in range(3):
            total = jnp.zeros((8, 128), F32)
            for b in range(3):
                if (side, t) in CROSS[b]:
                    pair = (b, 3 + t) if side > 0 else (t - 3, b)
                    total += result(b, CROSS[b].index((side, t))) * allowed(*pair)
            reto[i, t] = total

    relay(far).wait_recv()
    made, w = [sources(far)], [weights(far)]
    meet(made, w, (0,))
    meet(made, w, (256,), (2,))
    give(0, +1)
    pl.when(has_following)(lambda: give_back(0).start())
    meet(made, w, (256,), (0, 1))
    give(1, -1)
    pl.when(has_preceding)(lambda: give_back(1).start())

    def own_step(j, carry):
        chips = [order(2 * j + 1), order(2 * j + 2)]
        made = [[ft[o, 0], ft[o, 1]] for o in chips]
        meet(made, [weights(o) for o in chips], (512,))
        meet_rest(chips, made)
        return carry

    lax.fori_loop(0, nz // 2 - 1, own_step, 0)
    chips = [0, far]
    made = [[ft[o, 0], ft[o, 1]] for o in chips]
    meet(made, [weights(o) for o in chips], (512,))
    meet_rest(chips, made)

    sides(lambda: give_back(1).wait_recv(), lambda: give_back(0).wait_recv())
    inputs[3].wait()
    lane = lax.broadcasted_iota(jnp.int32, (8, 128), 1)
    packed = jnp.zeros((8, 128), F32)
    for t in range(3):
        total = reti[0, t] + reti[1, t]
        for b in range(3):
            if t < 2:
                r = result(b, 4 + t)
            else:
                top, lanes = 16 * (b % 2), pl.ds(128 * (b % 2), 128)
                r = accp[b // 2, top : top + 8, lanes] + accp[b // 2, top + 8 : top + 16, lanes]
            total += r if b == t else r * allowed(min(b, t), max(b, t))
        if t < 2:
            surface = accf[6:7, 128 * t : 128 * t + 128] + accf[14:15, 128 * t : 128 * t + 128]
        else:
            surface = accp[1, 22:23, 128:256] + accp[1, 30:31, 128:256]
        total += jnp.where(row8 == 0, surface, 0.0)
        pot[t] = total
        for k in range(3):
            an = bn[k, t : t + 1, :] * bp[3, t : t + 1, :]
            column = jnp.sum(total * an, axis=1, keepdims=True)
            packed = jnp.where(lane == 8 * (3 * t + k) + row8, column, packed)
    frc[s] = jnp.sum(packed, axis=0, keepdims=True)
    for d in range(1, tiles):
        forces(d, s).start()

    def velocity_step(j, carry):
        first, second = 0.0, 0.0
        for o in (2 * j, 2 * j + 1):
            lhs = []
            for b in range(3):
                tile = both(o, 24 if b < 2 else 32)
                w0 = jnp.broadcast_to(both(o, 8 * b)[0:1, :], (8, 256))
                lhs.append(split2(w0 * jnp.where(row == (7 if b == 1 else 3), 1.0, tile)))
            first += sweep(ft[o, 0], tgv[0], jnp.concatenate(lhs[:2], axis=0), cubed=True)
            second += sweep(ft[o, 1], tgv[1, :, 0:128], lhs[2], cubed=True)
        accv[...] += first
        accw[...] += second
        return carry

    lax.fori_loop(0, nz // 2, velocity_step, 0)

    v = [jnp.zeros((1, 128), F32)] * 3
    for b in range(3):
        ref = accv if b < 2 else accw
        top, lanes = 16 * (b % 2), pl.ds(128 * (b % 2), 128)
        moments = ref[top : top + 8, lanes] + ref[top + 8 : top + 16, lanes]
        r = 4 if b == 1 else 0
        point = (pay[0, 0, 36:37, :] + 2.0 * (1 - b), pay[0, 0, 37:38, :], DEPTH)
        for i in range(3):
            v[i] = v[i] + (moments[r + i : r + i + 1] - point[i] * moments[r + 3 : r + 4])
    inputs[4].wait()
    speed_sq = v[0] * v[0] + v[1] * v[1] + v[2] * v[2]
    phi, eta = fst[0:1, :], fst[1:2, :]
    fsn[0:1, :] = phi + STEP * (-GRAVITY * eta - 0.5 * speed_sq)
    fsn[1:2, :] = eta + STEP * v[2]

    for d in range(1, tiles):
        forces(0, lax.rem(s + d, tiles)).wait_recv()
    whole = frc[0]
    for i in range(1, tiles):
        whole = whole + frc[i]
    for t in range(3):
        for k in range(3):
            at = 8 * (3 * t + k)
            force[t, k : k + 1, :] = whole[:, at : at + 8]

    sides(lambda: points(0).wait_send(), lambda: points(1).wait_send())
    sides(lambda: give_back(0).wait_send(), lambda: give_back(1).wait_send())
    for o in range(nz):
        relay(o).wait_send()
        if o:
            direct(o).wait_send()
    for d in range(1, tiles):
        forces(d, s).wait_send()


def write_out(pot, force, fsn, pot_out, force_out, fsn_out):
    pot_out[...] = pot[...]
    force_out[...] = force[...]
    fsn_out[...] = fsn[...]


def on_device(bp, bn, fsp, fst, pairs):
    nz = lax.axis_size("surf") // 2
    tiles = 2 * nz
    dma = pltpu.SemaphoreType.DMA
    vmem = pl.BlockSpec(memory_space=pltpu.VMEM)
    shapes = (
        jax.ShapeDtypeStruct((3, 8, 128), F32),
        jax.ShapeDtypeStruct((3, 3, 8), F32),
        jax.ShapeDtypeStruct((2, 128), F32),
    )
    outs = pl.pallas_call(
        functools.partial(kernel, nz),
        out_shape=tuple(pltpu.VMEM(a.shape, a.dtype) for a in shapes),
        in_specs=[pl.BlockSpec(memory_space=pl.ANY)] * 5,
        out_specs=(vmem,) * 3,
        scratch_shapes=[
            pltpu.VMEM(bp.shape, F32),
            pltpu.VMEM(bn.shape, F32),
            pltpu.VMEM(fsp.shape, F32),
            pltpu.VMEM(fst.shape, F32),
            pltpu.VMEM(pairs.shape[::-1], jnp.int32),
            pltpu.VMEM((nz, 2, 40, 128), F32),
            pltpu.VMEM((2, 16, 128), F32),
            pltpu.VMEM((3, 48, 768), BF16),
            pltpu.VMEM((2, 48, 256), BF16),
            pltpu.VMEM((48, 256), BF16),
            pltpu.VMEM((2, 48, 256), BF16),
            pltpu.VMEM((nz, 2, 256, 48), BF16),
            pltpu.VMEM((3, 16, 768), F32),
            pltpu.VMEM((2, 32, 256), F32),
            pltpu.VMEM((16, 256), F32),
            pltpu.VMEM((32, 256), F32),
            pltpu.VMEM((16, 128), F32),
            pltpu.VMEM((2, 3, 8, 128), F32),
            pltpu.VMEM((2, 3, 8, 128), F32),
            pltpu.VMEM((16, 128), F32),
            pltpu.VMEM((tiles, 1, 128), F32),
            dma((5,)), dma((nz,)), dma((nz,)), dma((nz,)), dma((nz,)),
            dma((2,)), dma((2,)), dma((2,)), dma((2,)),
            dma((tiles,)), dma((tiles,)),
        ],
        compiler_params=pltpu.CompilerParams(collective_id=0, has_side_effects=True),
        name="section",
    )(bp, bn, fsp, fst, pairs.T)
    outs = [pltpu.with_memory_space_constraint(a, pltpu.VMEM) for a in outs]
    pot, force, fsn = pl.pallas_call(
        write_out, out_shape=shapes, in_specs=[vmem] * 3, out_specs=(vmem,) * 3, name="write_out"
    )(*outs)
    return pot, force.transpose(0, 2, 1), fsn


def solution(mesh):
    placed = (
        P(None, "body", "surf"),
        P(None, "body", "surf"),
        P(None, ("body", "surf")),
        P(None, ("body", "surf")),
        P(),
    )
    return jax.shard_map(
        on_device,
        mesh=mesh,
        in_specs=placed,
        out_specs=(P("body", None, "surf"), P("body", None, None), P(None, ("body", "surf"))),
        check_vma=False,
    )
```

```python
import functools

import jax
import jax.numpy as jnp
from jax import lax
from jax.experimental import pallas as pl
from jax.experimental.pallas import tpu as pltpu
from jax.sharding import PartitionSpec as P

MESH = pl.DeviceIdType.MESH
F32 = jnp.float32
BF16 = jnp.bfloat16
SOFTEN = 0.01
GRAVITY = 9.81
STEP = 0.2
DEPTH = 1.5

CROSS = [
    [(+1, t) for t in range(b + 1)] + [(-1, t) for t in range(b, 3)] for b in range(3)
]
PAIRS = [(0, 1), (0, 2), (1, 2)]
PAIRS += [(b, 3 + t) for b in range(3) for t in range(b + 1)]
PAIRS += [(t - 3, b) for b in range(3) for t in range(b, 3)]


def rounded(x):
    return x.astype(BF16).astype(F32)


def split3(x):
    a = rounded(x)
    r = x - a
    b = rounded(r)
    return a, b, rounded(r - b)


def split2(x):
    a = rounded(x)
    return jnp.concatenate([a, x - a], axis=0).astype(BF16)


def kernel(
    nz,
    bp_in, bn_in, fsp_in, fst_in, prs_in,
    pot, force, fsn,
    bp, bn, fsp, fst, prs,
    pay, nbr, tgt, tgp, tgf, tgv, ft, acc, accp, accf, accv, accw, reto, reti, msk, frc,
    s_in, s_dir, r_dir, s_rel, r_rel, s_nb, r_nb, s_ret, r_ret, s_f, r_f,
):
    groups = lax.axis_size("body")
    tiles = 2 * nz
    g = lax.axis_index("body")
    s = lax.axis_index("surf")
    z, core = s // 2, lax.rem(s, 2)
    partner = 2 * z + 1 - core
    following = lax.rem(g + 1, groups)
    preceding = lax.rem(g + groups - 1, groups)

    barrier = pltpu.get_barrier_semaphore()
    has_following, has_preceding = g < groups - 1, g > 0

    @pl.when(has_following)
    def _():
        pl.semaphore_signal(barrier, inc=1, device_id=(following, s), device_id_type=MESH)

    @pl.when(has_preceding)
    def _():
        pl.semaphore_signal(barrier, inc=1, device_id=(preceding, s), device_id_type=MESH)

    for d in sorted(range(1, tiles), key=lambda d: abs(d - nz)):
        pl.semaphore_signal(
            barrier, inc=1, device_id=(g, lax.rem(s + d, tiles)), device_id_type=MESH
        )

    inputs = [
        pltpu.make_async_copy(a, b, s_in.at[i])
        for i, (a, b) in enumerate(
            ((bp_in, bp), (fsp_in, fsp), (prs_in, prs), (bn_in, bn), (fst_in, fst))
        )
    ]
    for copy in inputs:
        copy.start()

    @pl.when(g == 0)
    def _():
        nbr[0] = jnp.zeros_like(nbr[0])
        reti[0] = jnp.zeros_like(reti[0])

    @pl.when(g == groups - 1)
    def _():
        nbr[1] = jnp.zeros_like(nbr[1])
        reti[1] = jnp.zeros_like(reti[1])

    inputs[0].wait()
    inputs[1].wait()

    base = 6.0 * g.astype(F32)
    area = bp[3]
    for k in range(8):
        w = bp[4 + k] * area
        for b in range(3):
            pay[0, 0, 8 * b + k : 8 * b + k + 1, :] = w[b : b + 1, :]
    for b in range(3):
        x = bp[0, b : b + 1, :] - (base + 2.0 * b)
        y = bp[1, b : b + 1, :]
        zz = bp[2, b : b + 1, :] + DEPTH
        for i, v in enumerate((x, y, zz, x * x + y * y + zz * zz)):
            pay[0, 0, 24 + 4 * b + i : 25 + 4 * b + i, :] = v
    fx = fsp[0:1, :] - (base + 2.0)
    fy = fsp[1:2, :]
    for i, v in enumerate((fx, fy, fsp[2:3, :] * fsp[3:4, :], fx * fx + fy * fy)):
        pay[0, 0, 36 + i : 37 + i, :] = v

    pl.semaphore_wait(
        barrier,
        tiles - 1 + (g + groups - 1) // groups + (2 * groups - 2 - g) // groups,
    )

    def direct(o):
        return pltpu.make_async_remote_copy(
            src_ref=pay.at[0, 0], dst_ref=pay.at[o, 0],
            send_sem=s_dir.at[o], recv_sem=r_dir.at[o],
            device_id=(g, 2 * lax.rem(z + o, nz) + core), device_id_type=MESH,
        )

    def relay(o):
        return pltpu.make_async_remote_copy(
            src_ref=pay.at[o, 0], dst_ref=pay.at[o, 1],
            send_sem=s_rel.at[o], recv_sem=r_rel.at[o],
            device_id=(g, partner), device_id_type=MESH,
        )

    far = nz // 2

    def across():
        return pltpu.make_async_remote_copy(
            src_ref=pay.at[0, 0], dst_ref=pay.at[far, 1],
            send_sem=s_rel.at[far], recv_sem=r_rel.at[far],
            device_id=(g, 2 * lax.rem(z + far, nz) + 1 - core), device_id_type=MESH,
        )

    def points(i):
        return pltpu.make_async_remote_copy(
            src_ref=pay.at[0, 0, pl.ds(24, 16)], dst_ref=nbr.at[i],
            send_sem=s_nb.at[i], recv_sem=r_nb.at[i],
            device_id=((following, preceding)[i], s), device_id_type=MESH,
        )

    def give_back(i):
        return pltpu.make_async_remote_copy(
            src_ref=reto.at[i], dst_ref=reti.at[i],
            send_sem=s_ret.at[i], recv_sem=r_ret.at[i],
            device_id=((following, preceding)[i], s), device_id_type=MESH,
        )

    def forces(d, slot):
        return pltpu.make_async_remote_copy(
            src_ref=frc.at[slot], dst_ref=frc.at[slot],
            send_sem=s_f.at[d], recv_sem=r_f.at[slot],
            device_id=(g, lax.rem(s + d, tiles)), device_id_type=MESH,
        )

    def order(k):
        half = (k + 1) // 2
        return jnp.where(lax.rem(k, 2) == 1, half, lax.rem(nz - half, nz))

    def sides(first, second):
        pl.when(has_following)(first)
        pl.when(has_preceding)(second)

    sides(lambda: points(0).start(), lambda: points(1).start())
    relay(0).start()
    for h in range(1, nz // 2 + 1):
        direct(h).start()
        if h != nz - h:
            direct(nz - h).start()
    inputs[2].wait()

    row_i = lax.broadcasted_iota(jnp.int32, (16, prs.shape[1]), 0)
    first = jnp.full(row_i.shape, -9, jnp.int32)
    second = first
    for r, (i, j) in enumerate(PAIRS):
        first = jnp.where(row_i == r, i, first)
        second = jnp.where(row_i == r, j, second)
    found = (prs[0:1, :] == first + 3 * g) & (prs[1:2, :] == second + 3 * g)
    hit = jnp.sum(jnp.where(found, 1.0, 0.0), axis=1, keepdims=True)
    msk[...] = jnp.broadcast_to(hit, (16, 128))

    def allowed(i, j):
        r = PAIRS.index((i, j))
        return jnp.broadcast_to(msk[r : r + 1, :], (8, 128))

    row8 = lax.broadcasted_iota(jnp.int32, (8, 128), 0)

    def put_target(ref, half, at, x, y, zz, use_z=True):
        m = x * x + y * y + zz * zz + SOFTEN
        r = jnp.where(row8 < 4, row8, row8 - 4)
        u = jnp.where(r == 0, -2.0 * x, jnp.where(r == 1, -2.0 * y, 0.0))
        if use_z:
            u = jnp.where(r == 2, -2.0 * zz, u)
        u = jnp.where(row8 == 3, 1.0, jnp.where(row8 == 7, m, u))
        u1, u2, u3 = split3(u)
        a = jnp.where((row8 < 4) | (row8 == 7), u1, u2)
        b = jnp.where(row8 == 7, u2, a)
        c = jnp.where((row8 < 3) | (row8 == 7), u3, u1)
        t = [a, b, c]
        zero = [jnp.zeros((8, 128), F32)] * 3
        t = t + zero if half == 0 else zero + t
        ref[:, 128 * at : 128 * at + 128] = jnp.concatenate(t, axis=0).astype(BF16)

    def spread(ref, r):
        return jnp.broadcast_to(ref[r : r + 1, :], (8, 128))

    def target(ref, b, at, points, r, shift):
        put_target(
            ref, b % 2, at, spread(points, r) + 2.0 * shift, spread(points, r + 1),
            spread(points, r + 2),
        )

    mine = pay.at[0, 0]
    for b in range(3):
        for t in range(2):
            target(tgt.at[b], b, 4 + t, mine, 24 + 4 * t, t - b)
        target(tgp.at[b // 2], b, b % 2, mine, 32, 2 - b)
        put_target(
            tgv.at[b // 2], b % 2, b % 2, spread(mine, 36) + 2.0 * (1 - b),
            spread(mine, 37), jnp.full((8, 128), DEPTH, F32),
        )
    for t in range(3):
        put_target(
            tgf if t < 2 else tgp.at[1], 1, t if t < 2 else 1,
            spread(mine, 24 + 4 * t) + 2.0 * (t - 1), spread(mine, 25 + 4 * t),
            spread(mine, 26 + 4 * t) - DEPTH, use_z=False,
        )

    for ref in (acc, accp, accf, accv, accw):
        ref[...] = jnp.zeros_like(ref)

    row = lax.broadcasted_iota(jnp.int32, (8, 256), 0)

    def both(o, r):
        return jnp.concatenate([pay[o, 0, r : r + 8, :], pay[o, 1, r : r + 8, :]], axis=1)

    def sources(o):
        made = []
        for i, p in enumerate((both(o, 24), both(o, 32))):
            q = pltpu.roll(p, 4, 0)
            groups = []
            for lo, hi in ((p, q), (q, p)):
                e = jnp.where(row < 4, lo, jnp.where(row < 7, hi, 1.0))
                e1, e2, e3 = split3(e)
                last = row == 7
                groups += [
                    e1, jnp.where(last, 1.0, e2),
                    jnp.where((row < 3) | last, e1, e3),
                ]
            made.append(jnp.concatenate(groups, axis=0).T.astype(BF16))
            ft[o, i] = made[i]
        return made

    def sweep(features, targets, lhs, cubed=False):
        his, los = [], []
        for c in range(2):
            d2 = jnp.dot(features[128 * c : 128 * c + 128, :], targets, preferred_element_type=F32)
            k = lax.rsqrt(d2)
            if cubed:
                k = k * k * k
            hi = k.astype(BF16)
            his.append(hi)
            los.append((k - hi.astype(F32)).astype(BF16))
        part = jnp.dot(lhs, jnp.concatenate(his, axis=0), preferred_element_type=F32)
        return part + jnp.dot(lhs, jnp.concatenate(los, axis=0), preferred_element_type=F32)

    def arrive(k):
        @pl.when(k < nz)
        def _():
            direct(order(k)).wait_recv()

        @pl.when(k < nz)
        def _():
            relay(order(k)).start()

    def weights(o):
        return [split2(both(o, 8 * b)) for b in range(3)]

    def meet(made, lhs, blocks, bodies=(0, 1, 2)):
        for b in bodies:
            for n in blocks:
                block = pl.ds(n, 256)
                acc[b, :, block] += sum(
                    sweep(f[b // 2], tgt[b, :, block], w[b]) for f, w in zip(made, lhs)
                )

    def meet_rest(chips, made):
        first, second, third = 0.0, 0.0, 0.0
        for o, f in zip(chips, made):
            surface = split2(both(o, 32))
            w = weights(o)
            first += sweep(f[0], tgp[0], jnp.concatenate([w[0], w[1]], axis=0))
            second += sweep(f[1], tgp[1], jnp.concatenate([w[2], surface], axis=0))
            third += sweep(f[1], tgf[...], surface)
        accp[0] += first
        accp[1] += second
        accf[...] += third

    def main_step(j, carry):
        arrive(2 * j + 3)
        arrive(2 * j + 4)
        chips = [order(2 * j + 1), order(2 * j + 2)]
        for o in chips:
            relay(o).wait_recv()
        meet([sources(o) for o in chips], [weights(o) for o in chips], (0, 256))
        return carry

    relay(0).wait_recv()
    made = sources(0)
    arrive(1)
    sides(lambda: points(1).wait_recv(), lambda: points(0).wait_recv())
    for b in range(3):
        for at, (side, t) in enumerate(CROSS[b]):
            target(tgt.at[b], b, at, nbr.at[0 if side < 0 else 1], 4 * t, 3 * side + t - b)

    arrive(2)
    meet([[ft[0, 0], ft[0, 1]]], [weights(0)], (0, 256))
    lax.fori_loop(0, nz // 2 - 1, main_step, 0)
    def result(b, at):
        lanes = pl.ds(128 * at, 128)
        return acc[b, 0:8, lanes] + acc[b, 8:16, lanes]

    def give(i, side):
        for t in range(3):
            total = jnp.zeros((8, 128), F32)
            for b in range(3):
                if (side, t) in CROSS[b]:
                    pair = (b, 3 + t) if side > 0 else (t - 3, b)
                    total += result(b, CROSS[b].index((side, t))) * allowed(*pair)
            reto[i, t] = total

    relay(far).wait_recv()
    made, w = [sources(far)], [weights(far)]
    meet(made, w, (0,))
    meet(made, w, (256,), (2,))
    give(0, +1)
    pl.when(has_following)(lambda: give_back(0).start())
    meet(made, w, (256,), (0, 1))
    give(1, -1)
    pl.when(has_preceding)(lambda: give_back(1).start())

    def own_step(j, carry):
        chips = [order(2 * j + 1), order(2 * j + 2)]
        made = [[ft[o, 0], ft[o, 1]] for o in chips]
        meet(made, [weights(o) for o in chips], (512,))
        meet_rest(chips, made)
        return carry

    lax.fori_loop(0, nz // 2 - 1, own_step, 0)
    chips = [0, far]
    made = [[ft[o, 0], ft[o, 1]] for o in chips]
    meet(made, [weights(o) for o in chips], (512,))
    meet_rest(chips, made)

    sides(lambda: give_back(1).wait_recv(), lambda: give_back(0).wait_recv())
    inputs[3].wait()
    lane = lax.broadcasted_iota(jnp.int32, (8, 128), 1)
    packed = jnp.zeros((8, 128), F32)
    for t in range(3):
        total = reti[0, t] + reti[1, t]
        for b in range(3):
            if t < 2:
                r = result(b, 4 + t)
            else:
                top, lanes = 16 * (b % 2), pl.ds(128 * (b % 2), 128)
                r = accp[b // 2, top : top + 8, lanes] + accp[b // 2, top + 8 : top + 16, lanes]
            total += r if b == t else r * allowed(min(b, t), max(b, t))
        if t < 2:
            surface = accf[6:7, 128 * t : 128 * t + 128] + accf[14:15, 128 * t : 128 * t + 128]
        else:
            surface = accp[1, 22:23, 128:256] + accp[1, 30:31, 128:256]
        total += jnp.where(row8 == 0, surface, 0.0)
        pot[t] = total
        for k in range(3):
            an = bn[k, t : t + 1, :] * bp[3, t : t + 1, :]
            column = jnp.sum(total * an, axis=1, keepdims=True)
            packed = jnp.where(lane == 8 * (3 * t + k) + row8, column, packed)
    frc[s] = jnp.sum(packed, axis=0, keepdims=True)
    for d in range(1, tiles):
        forces(d, s).start()

    def velocity_step(j, carry):
        first, second = 0.0, 0.0
        for o in (2 * j, 2 * j + 1):
            lhs = []
            for b in range(3):
                tile = both(o, 24 if b < 2 else 32)
                w0 = jnp.broadcast_to(both(o, 8 * b)[0:1, :], (8, 256))
                lhs.append(split2(w0 * jnp.where(row == (7 if b == 1 else 3), 1.0, tile)))
            first += sweep(ft[o, 0], tgv[0], jnp.concatenate(lhs[:2], axis=0), cubed=True)
            second += sweep(ft[o, 1], tgv[1, :, 0:128], lhs[2], cubed=True)
        accv[...] += first
        accw[...] += second
        return carry

    lax.fori_loop(0, nz // 2, velocity_step, 0)

    v = [jnp.zeros((1, 128), F32)] * 3
    for b in range(3):
        ref = accv if b < 2 else accw
        top, lanes = 16 * (b % 2), pl.ds(128 * (b % 2), 128)
        moments = ref[top : top + 8, lanes] + ref[top + 8 : top + 16, lanes]
        r = 4 if b == 1 else 0
        point = (pay[0, 0, 36:37, :] + 2.0 * (1 - b), pay[0, 0, 37:38, :], DEPTH)
        for i in range(3):
            v[i] = v[i] + (moments[r + i : r + i + 1] - point[i] * moments[r + 3 : r + 4])
    inputs[4].wait()
    speed_sq = v[0] * v[0] + v[1] * v[1] + v[2] * v[2]
    phi, eta = fst[0:1, :], fst[1:2, :]
    fsn[0:1, :] = phi + STEP * (-GRAVITY * eta - 0.5 * speed_sq)
    fsn[1:2, :] = eta + STEP * v[2]

    for d in range(1, tiles):
        forces(0, lax.rem(s + d, tiles)).wait_recv()
    whole = frc[0]
    for i in range(1, tiles):
        whole = whole + frc[i]
    for t in range(3):
        for k in range(3):
            at = 8 * (3 * t + k)
            force[t, k : k + 1, :] = whole[:, at : at + 8]

    sides(lambda: points(0).wait_send(), lambda: points(1).wait_send())
    sides(lambda: give_back(0).wait_send(), lambda: give_back(1).wait_send())
    for o in range(nz):
        relay(o).wait_send()
        if o:
            direct(o).wait_send()
    for d in range(1, tiles):
        forces(d, s).wait_send()


def write_out(pot, force, fsn, pot_out, force_out, fsn_out):
    pot_out[...] = pot[...]
    force_out[...] = force[...]
    fsn_out[...] = fsn[...]


def on_device(bp, bn, fsp, fst, pairs):
    nz = lax.axis_size("surf") // 2
    tiles = 2 * nz
    dma = pltpu.SemaphoreType.DMA
    vmem = pl.BlockSpec(memory_space=pltpu.VMEM)
    shapes = (
        jax.ShapeDtypeStruct((3, 8, 128), F32),
        jax.ShapeDtypeStruct((3, 3, 8), F32),
        jax.ShapeDtypeStruct((2, 128), F32),
    )
    outs = pl.pallas_call(
        functools.partial(kernel, nz),
        out_shape=tuple(pltpu.VMEM(a.shape, a.dtype) for a in shapes),
        in_specs=[pl.BlockSpec(memory_space=pl.ANY)] * 5,
        out_specs=(vmem,) * 3,
        scratch_shapes=[
            pltpu.VMEM(bp.shape, F32),
            pltpu.VMEM(bn.shape, F32),
            pltpu.VMEM(fsp.shape, F32),
            pltpu.VMEM(fst.shape, F32),
            pltpu.VMEM(pairs.shape[::-1], jnp.int32),
            pltpu.VMEM((nz, 2, 40, 128), F32),
            pltpu.VMEM((2, 16, 128), F32),
            pltpu.VMEM((3, 48, 768), BF16),
            pltpu.VMEM((2, 48, 256), BF16),
            pltpu.VMEM((48, 256), BF16),
            pltpu.VMEM((2, 48, 256), BF16),
            pltpu.VMEM((nz, 2, 256, 48), BF16),
            pltpu.VMEM((3, 16, 768), F32),
            pltpu.VMEM((2, 32, 256), F32),
            pltpu.VMEM((16, 256), F32),
            pltpu.VMEM((32, 256), F32),
            pltpu.VMEM((16, 128), F32),
            pltpu.VMEM((2, 3, 8, 128), F32),
            pltpu.VMEM((2, 3, 8, 128), F32),
            pltpu.VMEM((16, 128), F32),
            pltpu.VMEM((tiles, 1, 128), F32),
            dma((5,)), dma((nz,)), dma((nz,)), dma((nz,)), dma((nz,)),
            dma((2,)), dma((2,)), dma((2,)), dma((2,)),
            dma((tiles,)), dma((tiles,)),
        ],
        compiler_params=pltpu.CompilerParams(collective_id=0, has_side_effects=True),
        name="section",
    )(bp, bn, fsp, fst, pairs.T)
    outs = [pltpu.with_memory_space_constraint(a, pltpu.VMEM) for a in outs]
    pot, force, fsn = pl.pallas_call(
        write_out, out_shape=shapes, in_specs=[vmem] * 3, out_specs=(vmem,) * 3, name="write_out"
    )(*outs)
    return pot, force.transpose(0, 2, 1), fsn


def solution(mesh):
    placed = (
        P(None, "body", "surf"),
        P(None, "body", "surf"),
        P(None, ("body", "surf")),
        P(None, ("body", "surf")),
        P(),
    )
    return jax.shard_map(
        on_device,
        mesh=mesh,
        in_specs=placed,
        out_specs=(P("body", None, "surf"), P("body", None, None), P(None, ("body", "surf"))),
        check_vma=False,
    )
```
